512 devices in a mesh: rep: 4 (over z_lo), fsdp: 16 (over y, core), tp: 8 (over z_hi, x).
Axes of the slice: x: 4, y: 8, z: 8 (z_hi: 2, z_lo: 4; z = z_hi * 4 + z_lo), core: 2. Of those that a mesh axis runs over, the one named last changes fastest.
Arguments:
- delta_attn: float32 [4, 4, 768, 768], P('rep', None, 'fsdp', 'tp'), may hold values from -4 to 4
- delta_in: float32 [4, 768, 3072], P('rep', 'fsdp', 'tp'), may hold values from -4 to 4
- delta_out: float32 [4, 3072, 768], P('rep', 'fsdp', 'tp'), may hold values from -4 to 4
- delta_small: float32 [4, 1920], P('rep'), may hold values from -4 to 4
- emb_left: float32 [4, 8, 4016, 64], P('rep', 'tp', 'fsdp'), may hold values from -6 to 6
- emb_right: float32 [4, 64, 768], P('rep'), may hold values from -0.75 to 0.75
- anchor_attn: float32 [8, 294912], P('tp', 'fsdp'), may hold values from -6 to 6
- anchor_in: float32 [8, 294912], P('tp', 'fsdp'), may hold values from -6 to 6
- anchor_out: float32 [8, 294912], P('tp', 'fsdp'), may hold values from -6 to 6
- anchor_small: float32 [1920], P('fsdp'), may hold values from -6 to 6
- anchor_emb: float32 [8, 16, 4, 48192], P('tp', 'fsdp', 'rep'), may hold values from -6 to 6
- moment_attn: float32 [8, 294912], P('tp', 'fsdp'), may hold values from -4 to 4
- moment_in: float32 [8, 294912], P('tp', 'fsdp'), may hold values from -4 to 4
- moment_out: float32 [8, 294912], P('tp', 'fsdp'), may hold values from -4 to 4
- moment_small: float32 [1920], P('fsdp'), may hold values from -4 to 4
- moment_emb: float32 [8, 16, 4, 48192], P('tp', 'fsdp', 'rep'), may hold values from -4 to 4
Outputs:
- new_attn: float32 [4, 768, 768], P(None, 'fsdp', 'tp')
- new_in: float32 [768, 3072], P('fsdp', 'tp')
- new_out: float32 [3072, 768], P('fsdp', 'tp')
- new_small: float32 [1920], replicated
- new_emb: float32 [32128, 768], P('tp', 'fsdp')
- next_attn: float32 [8, 294912], P('tp', 'fsdp')
- next_in: float32 [8, 294912], P('tp', 'fsdp')
- next_out: float32 [8, 294912], P('tp', 'fsdp')
- next_small: float32 [1920], P('fsdp')
- next_emb: float32 [8, 16, 4, 48192], P('tp', 'fsdp', 'rep')
The draws below stay inside these ranges and needn't reach their ends.
All inputs are finite; a program needn't handle non-finite values.
Results may differ from the reference program's by a relative error of at most 0.000071.
Values sent between devices are 32-bit elements; how exact they have to be, the bound alone decides.
A program may use at most 64 MiB of HBM per device.

```python
import jax
import jax.numpy as jnp
from jax import lax

D = 768
FF = 3072
VOCAB = 32128
RANK = 64
SMALL = 1920
N_REP = 4
N_FSDP = 16
N_TP = 8


def levels(key, extent, cuts, smallest, largest):
    factor_of = 1.0
    for position, shards_of in cuts:
        draws = jax.random.uniform(jax.random.fold_in(jax.random.fold_in(key, 6), position), (shards_of,), jnp.float32, smallest / len(cuts), largest / len(cuts))
        factor_of = factor_of * jnp.repeat(jnp.exp(draws), extent[position] // shards_of).reshape((-1,) + (1,) * (len(extent) - 1 - position))
    return factor_of


def noise(rng, extent, scale, limit, shards=(), held_as=jnp.bfloat16):
    drawn = scale * jax.random.normal(rng, extent, jnp.float32)
    if shards:
        drawn = drawn * levels(rng, extent, shards, -0.22, 0.18)
    return jnp.clip(drawn, -limit, limit).astype(held_as)


def setup_inputs(seed: int = 0) -> dict:
    arg_keys = jax.random.split(jax.random.key(seed), 17)
    delta_attn = noise(arg_keys[0], (N_REP, 4, D, D), 0.5, 4.0, ((0, 4), (2, 16), (3, 8)), jnp.float32)
    delta_in = noise(arg_keys[1], (N_REP, D, FF), 0.5, 4.0, ((0, 4), (1, 16), (2, 8)), jnp.float32)
    delta_out = noise(arg_keys[2], (N_REP, FF, D), 0.5, 4.0, ((0, 4), (1, 16), (2, 8)), jnp.float32)
    delta_small = noise(arg_keys[3], (N_REP, SMALL), 0.5, 4.0, ((0, 4),), jnp.float32)
    emb_left = noise(arg_keys[4], (N_REP, N_TP, VOCAB // N_TP, RANK), 1.0, 6.0, ((0, 4), (1, 8), (2, 16)), jnp.float32)
    emb_right = noise(arg_keys[5], (N_REP, RANK, D), RANK ** -0.5, 0.75, ((0, 4),), jnp.float32)
    anchor_attn = noise(arg_keys[6], (N_TP, N_FSDP * 4 * D * (D // (N_TP * N_FSDP))), 1.0, 6.0, ((0, 8), (1, 16)), jnp.float32)
    anchor_in = noise(arg_keys[7], (N_TP, N_FSDP * D * (FF // (N_TP * N_FSDP))), 1.0, 6.0, ((0, 8), (1, 16)), jnp.float32)
    anchor_out = noise(arg_keys[8], (N_TP, N_FSDP * FF * (D // (N_TP * N_FSDP))), 1.0, 6.0, ((0, 8), (1, 16)), jnp.float32)
    anchor_small = noise(arg_keys[9], (SMALL,), 1.0, 6.0, ((0, 16),), jnp.float32)
    anchor_emb = noise(arg_keys[10], (N_TP, N_FSDP, N_REP, (VOCAB // (N_TP * N_FSDP)) * (D // N_REP)), 1.0, 6.0, ((0, 8), (1, 16), (2, 4)), jnp.float32)
    moment_attn = noise(arg_keys[11], (N_TP, N_FSDP * 4 * D * (D // (N_TP * N_FSDP))), 0.5, 4.0, ((0, 8), (1, 16)), jnp.float32)
    moment_in = noise(arg_keys[12], (N_TP, N_FSDP * D * (FF // (N_TP * N_FSDP))), 0.5, 4.0, ((0, 8), (1, 16)), jnp.float32)
    moment_out = noise(arg_keys[13], (N_TP, N_FSDP * FF * (D // (N_TP * N_FSDP))), 0.5, 4.0, ((0, 8), (1, 16)), jnp.float32)
    moment_small = noise(arg_keys[14], (SMALL,), 0.5, 4.0, ((0, 16),), jnp.float32)
    moment_emb = noise(arg_keys[15], (N_TP, N_FSDP, N_REP, (VOCAB // (N_TP * N_FSDP)) * (D // N_REP)), 0.5, 4.0, ((0, 8), (1, 16), (2, 4)), jnp.float32)
    return {"delta_attn": delta_attn, "delta_in": delta_in, "delta_out": delta_out, "delta_small": delta_small, "emb_left": emb_left, "emb_right": emb_right, "anchor_attn": anchor_attn, "anchor_in": anchor_in, "anchor_out": anchor_out, "anchor_small": anchor_small, "anchor_emb": anchor_emb, "moment_attn": moment_attn, "moment_in": moment_in, "moment_out": moment_out, "moment_small": moment_small, "moment_emb": moment_emb}


OUTER_RATE = 0.7
MOMENTUM_COEF = 0.9


def nesterov(anchor, moment, mean_delta):
    moment_next = MOMENTUM_COEF * moment + mean_delta
    updated = anchor - OUTER_RATE * (mean_delta + MOMENTUM_COEF * moment_next)
    return updated, moment_next


def unflat(flat, lead, rows, cols):
    width = cols // (N_TP * N_FSDP)
    shaped = flat.reshape(N_TP, N_FSDP, width, lead, rows)
    return jnp.transpose(shaped, (3, 4, 0, 1, 2)).reshape(lead, rows, cols)


def toflat(matrix, lead, rows, cols):
    width = cols // (N_TP * N_FSDP)
    shaped = matrix.reshape(lead, rows, N_TP, N_FSDP, width)
    return jnp.transpose(shaped, (2, 3, 4, 0, 1)).reshape(N_TP, N_FSDP * width * lead * rows)


def emb_unflat(flat):
    block_rows = VOCAB // (N_TP * N_FSDP)
    shaped = flat.reshape(N_TP, N_FSDP, N_REP, block_rows, D // N_REP)
    return jnp.transpose(shaped, (0, 1, 3, 2, 4)).reshape(VOCAB, D)


def emb_toflat(matrix):
    block_rows = VOCAB // (N_TP * N_FSDP)
    shaped = matrix.reshape(N_TP, N_FSDP, block_rows, N_REP, D // N_REP)
    return jnp.transpose(shaped, (0, 1, 3, 2, 4)).reshape(N_TP, N_FSDP, N_REP, block_rows * (D // N_REP))


def reference(delta_attn, delta_in, delta_out, delta_small, emb_left, emb_right, anchor_attn, anchor_in, anchor_out, anchor_small, anchor_emb, moment_attn, moment_in, moment_out, moment_small, moment_emb):
    mean_attn = jnp.sum(delta_attn, axis=0) / N_REP
    mean_in = jnp.sum(delta_in, axis=0) / N_REP
    mean_out = jnp.sum(delta_out, axis=0) / N_REP
    mean_small = jnp.sum(delta_small, axis=0) / N_REP
    left_cat = jnp.transpose(emb_left.reshape(N_REP, VOCAB, RANK), (1, 0, 2)).reshape(VOCAB, N_REP * RANK)
    right_cat = emb_right.reshape(N_REP * RANK, D)
    mean_emb = jnp.dot(left_cat, right_cat, precision=lax.Precision.HIGHEST, preferred_element_type=jnp.float32) / N_REP
    new_attn, next_attn = nesterov(unflat(anchor_attn, 4, D, D), unflat(moment_attn, 4, D, D), mean_attn)
    new_in, next_in = nesterov(unflat(anchor_in, 1, D, FF)[0], unflat(moment_in, 1, D, FF)[0], mean_in)
    new_out, next_out = nesterov(unflat(anchor_out, 1, FF, D)[0], unflat(moment_out, 1, FF, D)[0], mean_out)
    new_small, next_small = nesterov(anchor_small, moment_small, mean_small)
    new_emb, next_emb = nesterov(emb_unflat(anchor_emb), emb_unflat(moment_emb), mean_emb)
    return (new_attn, new_in, new_out, new_small, new_emb,
            toflat(next_attn, 4, D, D), toflat(next_in[None], 1, D, FF),
            toflat(next_out[None], 1, FF, D), next_small, emb_toflat(next_emb))
```

```python
import jax
import jax.numpy as jnp
from jax import lax
from jax.experimental import pallas as pl
from jax.experimental.pallas import tpu as pltpu
from jax.sharding import PartitionSpec as P

OUTER_RATE = 0.7
MOMENTUM_COEF = 0.9
G = 4
F = 16
ROWS = 251
KEEP = OUTER_RATE * MOMENTUM_COEF * MOMENTUM_COEF
STEP = OUTER_RATE * (1.0 + MOMENTUM_COEF) / G
MEAN = 1.0 / G


def dot(a, b, ca, cb):
    return lax.dot_general(
        a, b, (((ca,), (cb,)), ((), ())), precision=lax.Precision.HIGHEST, preferred_element_type=jnp.float32
    )


def sixth(d):
    return (d * 43) >> 8


def spread_rows():
    row = lax.broadcasted_iota(jnp.int32, (128, 96), 0)
    col = lax.broadcasted_iota(jnp.int32, (128, 96), 1)
    return (row == col + 2 * sixth(col)).astype(jnp.float32)


def pick_columns(q):
    row = lax.broadcasted_iota(jnp.int32, (384, 96), 0)
    col = lax.broadcasted_iota(jnp.int32, (384, 96), 1)
    return (row == col + 18 * sixth(col) + 6 * q).astype(jnp.float32)


def kernel(
    d_attn, d_in, d_out, d_small, left, right,
    a_attn, a_in, a_out, a_small, a_emb,
    m_attn, m_in, m_out, m_small, m_emb,
    new_attn, new_in, new_out, new_small, new_emb,
    next_attn, next_in, next_out, next_small, next_emb,
    lin, wide, widef, quart, quart_in, own_sum, sums, lpad, lt_own, lts, rts_own, rts, epad, et,
    amsg, arecv, umsg, urecv, gath,
    q_ss, q_rs, l_ss, l_rs, r_ss, r_rs, a_ss, a_rs, s_ss, s_rs, u_ss, u_rs, e_ss, up_ss, dn_ss, e_rs,
):
    f = lax.axis_index("fsdp")
    g = lax.axis_index("rep")

    def peer_f(d):
        return lax.rem(f + d, F)

    def peer_g(d):
        return lax.rem(g + d, G)

    bar = pltpu.get_barrier_semaphore()

    @pl.loop(1, F)
    def _(d):
        pl.semaphore_signal(bar, inc=1, device_id={"fsdp": peer_f(d)}, device_id_type=pl.DeviceIdType.MESH)

    @pl.loop(1, G)
    def _(d):
        pl.semaphore_signal(bar, inc=1, device_id={"rep": peer_g(d)}, device_id_type=pl.DeviceIdType.MESH)

    lpad[pl.ds(248, 8), :] = jnp.zeros((8, 64), jnp.float32)
    lpad[pl.ds(0, ROWS), :] = left[...]
    eye = (lax.broadcasted_iota(jnp.int32, (64, 64), 0) == lax.broadcasted_iota(jnp.int32, (64, 64), 1)).astype(jnp.float32)
    lt_own[...] = dot(eye, lpad[...], 1, 1)
    lts[g] = lt_own[...]
    for q in range(G):
        rts_own[q, :, 0:192] = right[:, q * 192 : (q + 1) * 192]
    rts[g] = rts_own[g]

    small = d_small[...]
    x_in = d_in[...]
    for q in range(G):
        quart[q, 0:48, 0:96] = d_attn[q * 48 : (q + 1) * 48, :]
        quart[q, 48:96, 0:96] = d_out[q * 48 : (q + 1) * 48, :]
        quart[q, 96:144, 0:96] = dot(x_in, pick_columns(q), 1, 0)
        quart[q, 144:160, 0:120] = small
    quart_in[g] = quart[g]

    pl.semaphore_wait(bar, F + G - 2)

    def left_copy(d):
        return pltpu.make_async_remote_copy(
            src_ref=lt_own, dst_ref=lts.at[g], send_sem=l_ss.at[d], recv_sem=l_rs.at[d],
            device_id={"rep": peer_g(d)}, device_id_type=pl.DeviceIdType.MESH)

    def right_copy(d):
        return pltpu.make_async_remote_copy(
            src_ref=rts_own.at[peer_g(d)], dst_ref=rts.at[g], send_sem=r_ss.at[d], recv_sem=r_rs.at[d],
            device_id={"rep": peer_g(d)}, device_id_type=pl.DeviceIdType.MESH)

    def quarter_copy(d):
        return pltpu.make_async_remote_copy(
            src_ref=quart.at[peer_g(d)], dst_ref=quart_in.at[g], send_sem=q_ss.at[d], recv_sem=q_rs.at[d],
            device_id={"rep": peer_g(d)}, device_id_type=pl.DeviceIdType.MESH)

    def sum_copy(d):
        return pltpu.make_async_remote_copy(
            src_ref=own_sum, dst_ref=sums.at[g], send_sem=s_ss.at[d], recv_sem=s_rs.at[d],
            device_id={"rep": peer_g(d)}, device_id_type=pl.DeviceIdType.MESH)

    def anchor_copy(d):
        return pltpu.make_async_remote_copy(
            src_ref=amsg.at[peer_f(d)], dst_ref=arecv.at[f], send_sem=a_ss.at[d], recv_sem=a_rs.at[d],
            device_id={"fsdp": peer_f(d)}, device_id_type=pl.DeviceIdType.MESH)

    def total_copy(d):
        return pltpu.make_async_remote_copy(
            src_ref=umsg.at[peer_f(d)], dst_ref=urecv.at[f], send_sem=u_ss.at[d], recv_sem=u_rs.at[d],
            device_id={"fsdp": peer_f(d)}, device_id_type=pl.DeviceIdType.MESH)

    def each(copy, n, what):
        @pl.loop(1, n)
        def _(d):
            getattr(copy(d), what)()

    each(left_copy, G, "start")
    each(right_copy, G, "start")
    each(quarter_copy, G, "start")

    amsg[...] = jnp.zeros((F, 8, 640), jnp.float32)
    lin[0] = a_attn[...] - KEEP * m_attn[...]
    lin[1] = a_out[...] - KEEP * m_out[...]
    lin[2] = a_in[...] - KEEP * m_in[...]
    for q in range(G):
        for s in range(6):
            wide[q, 0:6, s * 128 : (s + 1) * 128] = lin[0, pl.ds(q * 6 + s, 6, stride=24), :]
            wide[4 + q, 0:6, s * 128 : (s + 1) * 128] = lin[2, pl.ds(q * 36 + s, 6, stride=6), :]
    for s in range(24):
        widef[0:6, s * 128 : (s + 1) * 128] = lin[1, pl.ds(s, 6, stride=24), :]
    share = a_small[...] - KEEP * m_small[...]
    for t in range(F):
        for q in range(G):
            amsg[t, 0:6, q * 144 : q * 144 + 48] = wide[q, 0:6, t * 48 : (t + 1) * 48]
            amsg[t, 0:6, q * 144 + 48 : q * 144 + 96] = widef[0:6, t * 192 + q * 48 : t * 192 + q * 48 + 48]
            amsg[t, 0:6, q * 144 + 96 : q * 144 + 144] = wide[4 + q, 0:6, t * 48 : (t + 1) * 48]
        amsg[t, 6:7, 0:120] = share
    arecv[f] = amsg[f]
    each(anchor_copy, F, "start")

    each(left_copy, G, "wait_recv")
    each(right_copy, G, "wait_recv")
    u_emb = dot(lts[0], rts[0, :, 0:192], 0, 0)
    for k in range(1, G):
        u_emb = u_emb + dot(lts[k], rts[k, :, 0:192], 0, 0)
    u_emb = u_emb[0:ROWS, :]
    next_emb[...] = MOMENTUM_COEF * m_emb[...] + MEAN * u_emb
    epad[248:256, :] = jnp.zeros((8, 256), jnp.float32)
    epad[0:ROWS, 0:192] = a_emb[...] - KEEP * m_emb[...] - STEP * u_emb
    et[...] = jnp.transpose(epad[...])[0:192, :].reshape(4, 48, 256)

    def emb_copy(i):
        return pltpu.make_async_remote_copy(
            src_ref=et.at[i], dst_ref=gath.at[f], send_sem=e_ss.at[i], recv_sem=e_rs.at[f],
            device_id={"fsdp": g * 4 + i}, device_id_type=pl.DeviceIdType.MESH)

    plane = lax.div(f, 4)

    @pl.loop(0, 4)
    def _(i):
        @pl.when(f != g * 4 + i)
        def _():
            emb_copy(i).start()

    @pl.when(plane == g)
    def _():
        gath[f] = et[lax.rem(f, 4)]

    each(quarter_copy, G, "wait_recv")
    own_sum[...] = quart_in[0] + quart_in[1] + quart_in[2] + quart_in[3]
    sums[g] = own_sum[...]
    each(sum_copy, G, "start")
    each(sum_copy, G, "wait_recv")
    total = jnp.concatenate([sums[q, 0:144, 0:96] for q in range(G)], axis=0)
    spread = spread_rows()
    umsg[:, :, 0:576] = dot(spread, total, 1, 1).reshape(F, 8, 576)
    urecv[f] = umsg[f]
    each(total_copy, F, "start")

    up = jnp.logical_and(g >= plane, g < G - 1)
    down = jnp.logical_and(g <= plane, g > 0)

    def up_copy(s):
        return pltpu.make_async_remote_copy(
            src_ref=gath.at[s], dst_ref=gath.at[s], send_sem=up_ss.at[s], recv_sem=e_rs.at[s],
            device_id={"rep": jnp.minimum(g + 1, G - 1)}, device_id_type=pl.DeviceIdType.MESH)

    def down_copy(s):
        return pltpu.make_async_remote_copy(
            src_ref=gath.at[s], dst_ref=gath.at[s], send_sem=dn_ss.at[s], recv_sem=e_rs.at[s],
            device_id={"rep": jnp.maximum(g - 1, 0)}, device_id_type=pl.DeviceIdType.MESH)

    @pl.loop(0, F)
    def _(k):
        s = peer_f(k)

        @pl.when(jnp.logical_or(plane != g, s != f))
        def _():
            up_copy(s).wait_recv()

        @pl.when(up)
        def _():
            up_copy(s).start()

        @pl.when(down)
        def _():
            down_copy(s).start()

    each(anchor_copy, F, "wait_recv")
    fixed = dot(arecv[...].reshape(128, 640)[:, 0:576], spread, 0, 0)
    fresh = fixed - STEP * total
    acc = jnp.zeros((48, 384), jnp.float32)
    for q in range(G):
        new_attn[q * 48 : (q + 1) * 48, :] = fresh[q * 144 : q * 144 + 48, :]
        new_out[q * 48 : (q + 1) * 48, :] = fresh[q * 144 + 48 : q * 144 + 96, :]
        acc = acc + dot(fresh[q * 144 + 96 : q * 144 + 144, :], pick_columns(q), 1, 1)
    new_in[...] = acc
    for t in range(F):
        new_small[t : t + 1, :] = arecv[t, 6:7, 0:120] - STEP * own_sum[144 + t : 145 + t, 0:120]
    next_small[...] = MOMENTUM_COEF * m_small[...] + MEAN * own_sum[pl.ds(144 + f, 1), 0:120]

    each(total_copy, F, "wait_recv")
    for t in range(F):
        for q in range(G):
            wide[q, :, t * 48 : (t + 1) * 48] = urecv[t, :, q * 144 : q * 144 + 48]
            widef[:, t * 192 + q * 48 : t * 192 + q * 48 + 48] = urecv[t, :, q * 144 + 48 : q * 144 + 96]
            wide[4 + q, :, t * 48 : (t + 1) * 48] = urecv[t, :, q * 144 + 96 : q * 144 + 144]
    for q in range(G):
        for s in range(6):
            lin[0, pl.ds(q * 6 + s, 6, stride=24), :] = wide[q, 0:6, s * 128 : (s + 1) * 128]
            lin[2, pl.ds(q * 36 + s, 6, stride=6), :] = wide[4 + q, 0:6, s * 128 : (s + 1) * 128]
    for s in range(24):
        lin[1, pl.ds(s, 6, stride=24), :] = widef[0:6, s * 128 : (s + 1) * 128]
    next_attn[...] = MOMENTUM_COEF * m_attn[...] + MEAN * lin[0]
    next_out[...] = MOMENTUM_COEF * m_out[...] + MEAN * lin[1]
    next_in[...] = MOMENTUM_COEF * m_in[...] + MEAN * lin[2]

    for s in range(F):
        new_emb[s * ROWS : (s + 1) * ROWS, :] = jnp.transpose(gath[s])[0:ROWS, :]

    each(left_copy, G, "wait_send")
    each(right_copy, G, "wait_send")
    each(quarter_copy, G, "wait_send")
    each(sum_copy, G, "wait_send")
    each(anchor_copy, F, "wait_send")
    each(total_copy, F, "wait_send")

    @pl.loop(0, 4)
    def _(i):
        @pl.when(f != g * 4 + i)
        def _():
            emb_copy(i).wait_send()

    @pl.loop(0, F)
    def _(s):
        @pl.when(up)
        def _():
            up_copy(s).wait_send()

        @pl.when(down)
        def _():
            down_copy(s).wait_send()


def on_device(
    delta_attn, delta_in, delta_out, delta_small, emb_left, emb_right,
    anchor_attn, anchor_in, anchor_out, anchor_small, anchor_emb,
    moment_attn, moment_in, moment_out, moment_small, moment_emb,
):
    f32 = jnp.float32
    shape = lambda *s: jax.ShapeDtypeStruct(s, f32)
    vmem = pl.BlockSpec(memory_space=pltpu.VMEM)
    buf = lambda *s: pltpu.VMEM(s, f32)
    sem = lambda n: pltpu.SemaphoreType.DMA((n,))
    outs = pl.pallas_call(
        kernel,
        out_shape=(
            shape(192, 96), shape(48, 384), shape(192, 96), shape(16, 120), shape(4016, 48),
            shape(144, 128), shape(144, 128), shape(144, 128), shape(1, 120), shape(251, 192),
        ),
        in_specs=[vmem] * 16,
        out_specs=(vmem,) * 10,
        scratch_shapes=[
            buf(3, 144, 128), buf(8, 8, 768), buf(8, 3072),
            buf(4, 160, 128), buf(4, 160, 128), buf(160, 128), buf(4, 160, 128),
            buf(256, 64), buf(64, 256), buf(4, 64, 256), buf(4, 64, 256), buf(4, 64, 256),
            buf(256, 256), buf(4, 48, 256),
            buf(F, 8, 640), buf(F, 8, 640), buf(F, 8, 640), buf(F, 8, 640), buf(F, 48, 256),
            sem(G), sem(G), sem(G), sem(G), sem(G), sem(G), sem(F), sem(F), sem(G), sem(G), sem(F), sem(F),
            sem(4), sem(F), sem(F), sem(F),
        ],
        compiler_params=pltpu.CompilerParams(collective_id=0, has_side_effects=True, vmem_limit_bytes=48 * 2**20),
        name="outer_step",
    )(
        delta_attn.reshape(192, 96), delta_in[0], delta_out[0], delta_small.reshape(16, 120),
        emb_left[0, 0], emb_right[0],
        anchor_attn.reshape(144, 128), anchor_in.reshape(144, 128), anchor_out.reshape(144, 128),
        anchor_small[None, :], anchor_emb.reshape(251, 192),
        moment_attn.reshape(144, 128), moment_in.reshape(144, 128), moment_out.reshape(144, 128),
        moment_small[None, :], moment_emb.reshape(251, 192),
    )
    return (
        outs[0].reshape(4, 48, 96), outs[1], outs[2], outs[3].reshape(1920), outs[4],
        outs[5].reshape(1, 18432), outs[6].reshape(1, 18432), outs[7].reshape(1, 18432),
        outs[8].reshape(120), outs[9].reshape(1, 1, 1, 48192),
    )


def solution(mesh):
    placed = (
        P("rep", None, "fsdp", "tp"),
        P("rep", "fsdp", "tp"),
        P("rep", "fsdp", "tp"),
        P("rep", None),
        P("rep", "tp", "fsdp", None),
        P("rep", None, None),
        P("tp", "fsdp"),
        P("tp", "fsdp"),
        P("tp", "fsdp"),
        P("fsdp"),
        P("tp", "fsdp", "rep", None),
        P("tp", "fsdp"),
        P("tp", "fsdp"),
        P("tp", "fsdp"),
        P("fsdp"),
        P("tp", "fsdp", "rep", None),
    )
    return jax.shard_map(
        on_device,
        mesh=mesh,
        in_specs=placed,
        out_specs=(
            P(None, "fsdp", "tp"),
            P("fsdp", "tp"),
            P("fsdp", "tp"),
            P(),
            P("tp", "fsdp"),
            P("tp", "fsdp"),
            P("tp", "fsdp"),
            P("tp", "fsdp"),
            P("fsdp"),
            P("tp", "fsdp", "rep", None),
        ),
        check_vma=False,
    )
```

```python
import jax
import jax.numpy as jnp
from jax import lax
from jax.experimental import pallas as pl
from jax.experimental.pallas import tpu as pltpu
from jax.sharding import PartitionSpec as P

OUTER_RATE = 0.7
MOMENTUM_COEF = 0.9
G = 4
F = 16
ROWS = 251
KEEP = OUTER_RATE * MOMENTUM_COEF * MOMENTUM_COEF
STEP = OUTER_RATE * (1.0 + MOMENTUM_COEF) / G
MEAN = 1.0 / G


def dot(a, b, ca, cb):
    return lax.dot_general(
        a, b, (((ca,), (cb,)), ((), ())), precision=lax.Precision.HIGHEST, preferred_element_type=jnp.float32
    )


def sixth(d):
    return (d * 43) >> 8


def spread_rows():
    row = lax.broadcasted_iota(jnp.int32, (128, 96), 0)
    col = lax.broadcasted_iota(jnp.int32, (128, 96), 1)
    return (row == col + 2 * sixth(col)).astype(jnp.float32)


def pick_columns(q):
    row = lax.broadcasted_iota(jnp.int32, (384, 96), 0)
    col = lax.broadcasted_iota(jnp.int32, (384, 96), 1)
    return (row == col + 18 * sixth(col) + 6 * q).astype(jnp.float32)


def kernel(
    d_attn_h, d_in_h, d_out_h, d_small_h, left_h, right_h,
    a_attn_h, a_in_h, a_out_h, a_small_h, a_emb_h,
    m_attn_h, m_in_h, m_out_h, m_small_h, m_emb_h,
    new_attn_h, new_in_h, new_out_h, new_small_h, new_emb_h,
    next_attn_h, next_in_h, next_out_h, next_small_h, next_emb_h,
    new_attn, new_in, new_out, new_small, new_emb,
    next_attn, next_in, next_out, next_small, next_emb,
    d_attn, d_in, d_out, d_small, right,
    a_attn, a_in, a_out, a_small, a_emb,
    m_attn, m_in, m_out, m_small, m_emb,
    flat_small, lin, wide, widef, quart, quart_in, own_sum, sums, tot, lts, rts_own, rts, base, un, et,
    amsg, arecv, umsg, urecv, gath,
    in_s, out_s, q_ss, q_rs, l_ss, l_rs, r_ss, r_rs, x_ss, x_rs, a_ss, a_rs, s_ss, s_rs, u_ss, u_rs, e_ss, up_ss, dn_ss, e_rs,
):
    f = lax.axis_index("fsdp")
    g = lax.axis_index("rep")
    c = lax.rem(f, 2)

    def peer_f(d):
        return lax.rem(f + d, F)

    def peer_g(d):
        return lax.rem(g + d, G)

    loads = [
        pltpu.make_async_copy(src, dst, in_s.at[i])
        for i, (src, dst) in enumerate((
            (left_h, lts.at[g]), (right_h, right), (d_in_h, d_in), (d_attn_h, d_attn), (d_out_h, d_out),
            (d_small_h, d_small), (a_attn_h, a_attn), (m_attn_h, m_attn), (a_out_h, a_out), (m_out_h, m_out),
            (a_in_h, a_in), (m_in_h, m_in), (a_small_h, a_small), (m_small_h, m_small), (a_emb_h, a_emb),
            (m_emb_h, m_emb),
        ))
    ]
    for load in loads:
        load.start()
    stores = [
        pltpu.make_async_copy(src, dst, out_s.at[i])
        for i, (src, dst) in enumerate((
            (new_attn, new_attn_h), (new_in, new_in_h), (new_out, new_out_h), (new_small, new_small_h),
            (new_emb, new_emb_h), (next_attn, next_attn_h), (next_in, next_in_h), (next_out, next_out_h),
            (next_small, next_small_h), (next_emb, next_emb_h),
        ))
    ]

    bar = pltpu.get_barrier_semaphore()

    @pl.loop(1, F)
    def _(d):
        pl.semaphore_signal(bar, inc=1, device_id={"fsdp": peer_f(d)}, device_id_type=pl.DeviceIdType.MESH)

    @pl.loop(1, G)
    def _(d):
        pl.semaphore_signal(bar, inc=1, device_id={"rep": peer_g(d)}, device_id_type=pl.DeviceIdType.MESH)

    for load in loads[:6]:
        load.wait()
    for q in range(G):
        for h in range(2):
            rts_own[q, h, :, 0:192] = right[h * 32 : (h + 1) * 32, q * 192 : (q + 1) * 192]
    rts[g] = rts_own[g]

    for t in range(F):
        quart[0, 112 + t : 113 + t, 0:120] = d_small[:, t * 120 : (t + 1) * 120]
    small = quart[0, 112:128, 0:120]
    x_in = d_in[...]
    for q in range(G):
        x_q = dot(x_in, pick_columns(q), 1, 0)
        quart[q, 0:48, 0:96] = d_attn[q * 48 : (q + 1) * 48, :]
        quart[q, 0:48, 96:128] = x_q[:, 0:32]
        quart[q, 48:96, 0:96] = d_out[q * 48 : (q + 1) * 48, :]
        quart[q, 48:96, 96:128] = x_q[:, 32:64]
        for b in range(3):
            quart[q, 96:112, b * 32 : (b + 1) * 32] = x_q[b * 16 : (b + 1) * 16, 64:96]
        if q:
            quart[q, 112:128, 0:120] = small
    quart_in[g] = quart[g]

    pl.semaphore_wait(bar, F + G - 2)

    def rep_copy(src, dst, ss, rs, d):
        return pltpu.make_async_remote_copy(
            src_ref=src, dst_ref=dst, send_sem=ss.at[d], recv_sem=rs.at[d],
            device_id={"rep": peer_g(d)}, device_id_type=pl.DeviceIdType.MESH)

    def left_copy(d):
        return rep_copy(lts.at[g], lts.at[g], l_ss, l_rs, d)

    def right_copy(d):
        return rep_copy(rts_own.at[peer_g(d), c], rts.at[g, c], r_ss, r_rs, d)

    def quarter_copy(d):
        return rep_copy(quart.at[peer_g(d)], quart_in.at[g], q_ss, q_rs, d)

    def sum_copy(d):
        return rep_copy(own_sum.at[pl.ds(0, 112)], sums.at[g], s_ss, s_rs, d)

    def half_copy(d):
        part = rts.at[peer_g(G - d), c]
        return pltpu.make_async_remote_copy(
            src_ref=part, dst_ref=part, send_sem=x_ss.at[d], recv_sem=x_rs.at[d],
            device_id={"fsdp": f + 1 - 2 * c}, device_id_type=pl.DeviceIdType.MESH)

    def anchor_copy(d):
        return pltpu.make_async_remote_copy(
            src_ref=amsg.at[peer_f(d)], dst_ref=arecv.at[f], send_sem=a_ss.at[d], recv_sem=a_rs.at[d],
            device_id={"fsdp": peer_f(d)}, device_id_type=pl.DeviceIdType.MESH)

    def total_copy(d):
        return pltpu.make_async_remote_copy(
            src_ref=umsg.at[peer_f(d)], dst_ref=urecv.at[f], send_sem=u_ss.at[d], recv_sem=u_rs.at[d],
            device_id={"fsdp": peer_f(d)}, device_id_type=pl.DeviceIdType.MESH)

    def each(copy, n, what):
        @pl.loop(1, n)
        def _(d):
            getattr(copy(d), what)()

    each(right_copy, G, "start")
    each(left_copy, G, "start")
    each(quarter_copy, G, "start")

    for load in loads[6:]:
        load.wait()

    @pl.loop(0, 125, unroll=5)
    def _(p):
        at = pl.ds(pl.multiple_of(p * 384, 128), 384)
        x = a_emb[:, at] - KEEP * m_emb[:, at]
        base[pl.ds(2 * p, 1), 0:192] = x[:, 0:192]
        base[pl.ds(2 * p + 1, 1), 0:192] = x[:, 192:384]

    base[250:251, 0:192] = a_emb[:, 48000:48192] - KEEP * m_emb[:, 48000:48192]

    @pl.loop(1, G)
    def _(d):
        right_copy(d).wait_recv()
        half_copy(d).start()

    amsg[...] = jnp.zeros((F, 8, 640), jnp.float32)
    lin[0] = a_attn[...] - KEEP * m_attn[...]
    lin[1] = a_out[...] - KEEP * m_out[...]
    lin[2] = a_in[...] - KEEP * m_in[...]
    for q in range(G):
        for s in range(6):
            wide[q, 0:6, s * 128 : (s + 1) * 128] = lin[0, pl.ds(q * 6 + s, 6, stride=24), :]
            wide[4 + q, 0:6, s * 128 : (s + 1) * 128] = lin[2, pl.ds(q * 36 + s, 6, stride=6), :]
    for s in range(24):
        widef[0:6, s * 128 : (s + 1) * 128] = lin[1, pl.ds(s, 6, stride=24), :]
    share = a_small[...] - KEEP * m_small[...]
    for t in range(F):
        for q in range(G):
            amsg[t, 0:6, q * 144 : q * 144 + 48] = wide[q, 0:6, t * 48 : (t + 1) * 48]
            amsg[t, 0:6, q * 144 + 48 : q * 144 + 96] = widef[0:6, t * 192 + q * 48 : t * 192 + q * 48 + 48]
            amsg[t, 0:6, q * 144 + 96 : q * 144 + 144] = wide[4 + q, 0:6, t * 48 : (t + 1) * 48]
        amsg[t, 6:7, 0:120] = share
    arecv[f] = amsg[f]
    each(anchor_copy, F, "start")

    each(left_copy, G, "wait_recv")
    each(half_copy, G, "wait_recv")
    u_emb = dot(lts[...].reshape(256, ROWS), rts[...].reshape(256, 256)[:, 0:192], 0, 0)
    un[0:ROWS, 0:192] = u_emb
    base[0:ROWS, 0:192] = base[0:ROWS, 0:192] - STEP * u_emb
    et[...] = jnp.transpose(base[...])[0:192, 0:ROWS].reshape(4, 48, ROWS)

    def emb_copy(i):
        return pltpu.make_async_remote_copy(
            src_ref=et.at[i], dst_ref=gath.at[f], send_sem=e_ss.at[i], recv_sem=e_rs.at[f],
            device_id={"fsdp": g * 4 + i}, device_id_type=pl.DeviceIdType.MESH)

    plane = lax.div(f, 4)

    @pl.loop(0, 4)
    def _(i):
        @pl.when(f != g * 4 + i)
        def _():
            emb_copy(i).start()

    @pl.when(plane == g)
    def _():
        gath[f] = et[lax.rem(f, 4)]

    each(quarter_copy, G, "wait_recv")
    own_sum[...] = quart_in[0] + quart_in[1] + quart_in[2] + quart_in[3]
    sums[g] = own_sum[0:112, :]
    each(sum_copy, G, "start")

    @pl.loop(0, 125, unroll=5)
    def _(p):
        at = pl.ds(pl.multiple_of(p * 384, 128), 384)
        x = jnp.concatenate([un[pl.ds(2 * p, 1), 0:192], un[pl.ds(2 * p + 1, 1), 0:192]], axis=1)
        next_emb[:, at] = MOMENTUM_COEF * m_emb[:, at] + MEAN * x

    next_emb[:, 48000:48192] = MOMENTUM_COEF * m_emb[:, 48000:48192] + MEAN * un[250:251, 0:192]
    stores[9].start()

    each(sum_copy, G, "wait_recv")
    for q in range(G):
        tot[q, 0:96, 0:96] = sums[q, 0:96, 0:96]
        tot[q, 96:144, 0:32] = sums[q, 0:48, 96:128]
        tot[q, 96:144, 32:64] = sums[q, 48:96, 96:128]
        for b in range(3):
            tot[q, 96 + b * 16 : 112 + b * 16, 64:96] = sums[q, 96:112, b * 32 : (b + 1) * 32]
    total = tot[...].reshape(576, 128)[:, 0:96]
    spread = spread_rows()
    umsg[:, :, 0:576] = dot(spread, total, 1, 1).reshape(F, 8, 576)
    urecv[f] = umsg[f]
    each(total_copy, F, "start")

    up = jnp.logical_and(g >= plane, g < G - 1)
    down = jnp.logical_and(g <= plane, g > 0)

    def up_copy(s):
        return pltpu.make_async_remote_copy(
            src_ref=gath.at[s], dst_ref=gath.at[s], send_sem=up_ss.at[s], recv_sem=e_rs.at[s],
            device_id={"rep": jnp.minimum(g + 1, G - 1)}, device_id_type=pl.DeviceIdType.MESH)

    def down_copy(s):
        return pltpu.make_async_remote_copy(
            src_ref=gath.at[s], dst_ref=gath.at[s], send_sem=dn_ss.at[s], recv_sem=e_rs.at[s],
            device_id={"rep": jnp.maximum(g - 1, 0)}, device_id_type=pl.DeviceIdType.MESH)

    def relay(lo, hi):
        @pl.loop(lo, hi)
        def _(k):
            s = peer_f(k)

            @pl.when(jnp.logical_or(plane != g, s != f))
            def _():
                up_copy(s).wait_recv()

            @pl.when(up)
            def _():
                up_copy(s).start()

            @pl.when(down)
            def _():
                down_copy(s).start()

    relay(0, 6)

    each(anchor_copy, F, "wait_recv")
    fixed = dot(arecv[...].reshape(128, 640)[:, 0:576], spread, 0, 0)
    fresh = fixed - STEP * total
    acc = jnp.zeros((48, 384), jnp.float32)
    for q in range(G):
        new_attn[q * 48 : (q + 1) * 48, :] = fresh[q * 144 : q * 144 + 48, :]
        new_out[q * 48 : (q + 1) * 48, :] = fresh[q * 144 + 48 : q * 144 + 96, :]
        acc = acc + dot(fresh[q * 144 + 96 : q * 144 + 144, :], pick_columns(q), 1, 1)
    new_in[...] = acc
    for t in range(F):
        flat_small[:, t * 120 : (t + 1) * 120] = arecv[t, 6:7, 0:120] - STEP * own_sum[112 + t : 113 + t, 0:120]
    for t in range(15):
        new_small[t : t + 1, :] = flat_small[:, t * 128 : (t + 1) * 128]
    next_small[...] = MOMENTUM_COEF * m_small[...] + MEAN * own_sum[pl.ds(112 + f, 1), 0:120]
    for i in (0, 1, 2, 3, 8):
        stores[i].start()

    relay(6, 11)

    each(total_copy, F, "wait_recv")
    for t in range(F):
        for q in range(G):
            wide[q, :, t * 48 : (t + 1) * 48] = urecv[t, :, q * 144 : q * 144 + 48]
            widef[:, t * 192 + q * 48 : t * 192 + q * 48 + 48] = urecv[t, :, q * 144 + 48 : q * 144 + 96]
            wide[4 + q, :, t * 48 : (t + 1) * 48] = urecv[t, :, q * 144 + 96 : q * 144 + 144]
    for q in range(G):
        for s in range(6):
            lin[0, pl.ds(q * 6 + s, 6, stride=24), :] = wide[q, 0:6, s * 128 : (s + 1) * 128]
            lin[2, pl.ds(q * 36 + s, 6, stride=6), :] = wide[4 + q, 0:6, s * 128 : (s + 1) * 128]
    for s in range(24):
        lin[1, pl.ds(s, 6, stride=24), :] = widef[0:6, s * 128 : (s + 1) * 128]
    next_attn[...] = MOMENTUM_COEF * m_attn[...] + MEAN * lin[0]
    next_out[...] = MOMENTUM_COEF * m_out[...] + MEAN * lin[1]
    next_in[...] = MOMENTUM_COEF * m_in[...] + MEAN * lin[2]
    for i in (5, 6, 7):
        stores[i].start()

    relay(11, F)
    for s in range(F):
        new_emb[:, s * ROWS : (s + 1) * ROWS] = gath[s]
    stores[4].start()

    each(left_copy, G, "wait_send")
    each(right_copy, G, "wait_send")
    each(half_copy, G, "wait_send")
    each(quarter_copy, G, "wait_send")
    each(sum_copy, G, "wait_send")
    each(anchor_copy, F, "wait_send")
    each(total_copy, F, "wait_send")

    @pl.loop(0, 4)
    def _(i):
        @pl.when(f != g * 4 + i)
        def _():
            emb_copy(i).wait_send()

    @pl.loop(0, F)
    def _(s):
        @pl.when(up)
        def _():
            up_copy(s).wait_send()

        @pl.when(down)
        def _():
            down_copy(s).wait_send()

    for store in stores:
        store.wait()


def write_out(*refs):
    n = (len(refs) - 2) // 3
    took, gave = refs[3 * n], refs[3 * n + 1]
    inward = [pltpu.make_async_copy(refs[i], refs[2 * n + i], took.at[i]) for i in range(n)]
    outward = [pltpu.make_async_copy(refs[2 * n + i], refs[n + i], gave.at[i]) for i in range(n)]
    for copy in inward:
        copy.start()
    for i in range(n):
        inward[i].wait()
        outward[i].start()
    for copy in outward:
        copy.wait()


def on_device(
    delta_attn, delta_in, delta_out, delta_small, emb_left, emb_right,
    anchor_attn, anchor_in, anchor_out, anchor_small, anchor_emb,
    moment_attn, moment_in, moment_out, moment_small, moment_emb,
):
    f32 = jnp.float32
    shape = lambda *s: jax.ShapeDtypeStruct(s, f32)
    hbm = pl.BlockSpec(memory_space=pltpu.HBM)
    buf = lambda *s: pltpu.VMEM(s, f32)
    sem = lambda n: pltpu.SemaphoreType.DMA((n,))
    results = (
        shape(192, 96), shape(48, 384), shape(192, 96), shape(15, 128), shape(48, 4016),
        shape(144, 128), shape(144, 128), shape(144, 128), shape(1, 120), shape(1, 48192),
    )
    held = pl.pallas_call(
        kernel,
        out_shape=results,
        in_specs=[hbm] * 16,
        out_specs=(hbm,) * 10,
        scratch_shapes=[
            *(pltpu.VMEM(r.shape, f32) for r in results),
            buf(192, 96), buf(48, 384), buf(192, 96), buf(1, 1920), buf(64, 768),
            buf(144, 128), buf(144, 128), buf(144, 128), buf(1, 120), buf(1, 48192),
            buf(144, 128), buf(144, 128), buf(144, 128), buf(1, 120), buf(1, 48192),
            buf(1, 1920), buf(3, 144, 128), buf(8, 8, 768), buf(8, 3072),
            buf(4, 128, 128), buf(4, 128, 128), buf(128, 128), buf(4, 112, 128), buf(4, 144, 128),
            buf(4, 64, ROWS), buf(4, 2, 32, 256), buf(4, 2, 32, 256),
            buf(256, 256), buf(256, 256), buf(4, 48, ROWS),
            buf(F, 8, 640), buf(F, 8, 640), buf(F, 8, 640), buf(F, 8, 640), buf(F, 48, ROWS),
            sem(16), sem(10), sem(G), sem(G), sem(G), sem(G), sem(G), sem(G), sem(G), sem(G), sem(F), sem(F), sem(G), sem(G),
            sem(F), sem(F), sem(4), sem(F), sem(F), sem(F),
        ],
        compiler_params=pltpu.CompilerParams(collective_id=0, has_side_effects=True, vmem_limit_bytes=60 * 2**20),
        name="outer_step",
    )(
        delta_attn.reshape(192, 96), delta_in[0], delta_out[0], delta_small, emb_left[0, 0].T, emb_right[0],
        anchor_attn.reshape(144, 128), anchor_in.reshape(144, 128), anchor_out.reshape(144, 128),
        anchor_small.reshape(1, 120), anchor_emb.reshape(1, 48192),
        moment_attn.reshape(144, 128), moment_in.reshape(144, 128), moment_out.reshape(144, 128),
        moment_small.reshape(1, 120), moment_emb.reshape(1, 48192),
    )
    outs = pl.pallas_call(
        write_out,
        out_shape=results,
        in_specs=[hbm] * 10,
        out_specs=(hbm,) * 10,
        scratch_shapes=[*(pltpu.VMEM(r.shape, f32) for r in results), sem(10), sem(10)],
        compiler_params=pltpu.CompilerParams(vmem_limit_bytes=60 * 2**20),
        name="write_out",
    )(*held)
    return (
        outs[0].reshape(4, 48, 96), outs[1], outs[2], outs[3].reshape(1920), outs[4].T,
        outs[5].reshape(1, 18432), outs[6].reshape(1, 18432), outs[7].reshape(1, 18432),
        outs[8].reshape(120), outs[9].reshape(1, 1, 1, 48192),
    )


def solution(mesh):
    placed = (
        P("rep", None, "fsdp", "tp"),
        P("rep", "fsdp", "tp"),
        P("rep", "fsdp", "tp"),
        P("rep", None),
        P("rep", "tp", "fsdp", None),
        P("rep", None, None),
        P("tp", "fsdp"),
        P("tp", "fsdp"),
        P("tp", "fsdp"),
        P("fsdp"),
        P("tp", "fsdp", "rep", None),
        P("tp", "fsdp"),
        P("tp", "fsdp"),
        P("tp", "fsdp"),
        P("fsdp"),
        P("tp", "fsdp", "rep", None),
    )
    return jax.shard_map(
        on_device,
        mesh=mesh,
        in_specs=placed,
        out_specs=(
            P(None, "fsdp", "tp"),
            P("fsdp", "tp"),
            P("fsdp", "tp"),
            P(),
            P("tp", "fsdp"),
            P("tp", "fsdp"),
            P("tp", "fsdp"),
            P("tp", "fsdp"),
            P("fsdp"),
            P("tp", "fsdp", "rep", None),
        ),
        check_vma=False,
    )
```

```python
import jax
import jax.numpy as jnp
from jax import lax
from jax.experimental import pallas as pl
from jax.experimental.pallas import tpu as pltpu
from jax.sharding import PartitionSpec as P

OUTER_RATE = 0.7
MOMENTUM_COEF = 0.9
G = 4
F = 16
ROWS = 251
KEEP = OUTER_RATE * MOMENTUM_COEF * MOMENTUM_COEF
STEP = OUTER_RATE * (1.0 + MOMENTUM_COEF) / G
MEAN = 1.0 / G


def dot(a, b, ca, cb):
    return lax.dot_general(
        a, b, (((ca,), (cb,)), ((), ())), precision=lax.Precision.HIGHEST, preferred_element_type=jnp.float32
    )


def sixth(d):
    return (d * 43) >> 8


def spread_rows():
    row = lax.broadcasted_iota(jnp.int32, (128, 96), 0)
    col = lax.broadcasted_iota(jnp.int32, (128, 96), 1)
    return (row == col + 2 * sixth(col)).astype(jnp.float32)


def pick_columns(q):
    row = lax.broadcasted_iota(jnp.int32, (384, 96), 0)
    col = lax.broadcasted_iota(jnp.int32, (384, 96), 1)
    return (row == col + 18 * sixth(col) + 6 * q).astype(jnp.float32)


def kernel(
    d_attn_h, d_in_h, d_out_h, d_small_h, left_h, right_h,
    a_attn_h, a_in_h, a_out_h, a_small_h, a_emb_h,
    m_attn_h, m_in_h, m_out_h, m_small_h, m_emb_h,
    new_attn_h, new_in_h, new_out_h, new_small_h, new_emb_h,
    next_attn_h, next_in_h, next_out_h, next_small_h, next_emb_h,
    new_attn, new_in, new_out, new_small, new_emb,
    next_attn, next_in, next_out, next_small, next_emb,
    d_attn, d_in, d_out, d_small, right,
    a_attn, a_in, a_out, a_small, a_emb,
    m_attn, m_in, m_out, m_small, m_emb,
    flat_small, lin, wide, widef, quart, quart_in, own_sum, sums, tot, lts, rts_own, rts, base, un, et,
    amsg, arecv, umsg, urecv, gath,
    in_s, out_s, q_ss, q_rs, lu_ss, ld_ss, l_rs, r_ss, r_rs, x_ss, x_rs, a_ss, a_rs, su_ss, sd_ss, s_rs, u_ss, u_rs, e_ss, up_ss, dn_ss, e_rs,
):
    f = lax.axis_index("fsdp")
    g = lax.axis_index("rep")
    tp = lax.axis_index("tp")
    c = lax.rem(f, 2)
    x = lax.rem(tp, 4)
    part = 2 * x + c

    def peer_f(d):
        return lax.rem(f + d, F)

    def peer_g(d):
        return lax.rem(g + d, G)

    loads = [
        pltpu.make_async_copy(src, dst, in_s.at[i])
        for i, (src, dst) in enumerate((
            (left_h, lts.at[g]), (right_h, right), (d_in_h, d_in), (d_attn_h, d_attn), (d_out_h, d_out),
            (d_small_h, d_small), (a_attn_h, a_attn), (m_attn_h, m_attn), (a_out_h, a_out), (m_out_h, m_out),
            (a_in_h, a_in), (m_in_h, m_in), (a_small_h, a_small), (m_small_h, m_small), (a_emb_h, a_emb),
            (m_emb_h, m_emb),
        ))
    ]
    for load in loads:
        load.start()
    stores = [
        pltpu.make_async_copy(src, dst, out_s.at[i])
        for i, (src, dst) in enumerate((
            (new_attn, new_attn_h), (new_in, new_in_h), (new_out, new_out_h), (new_small, new_small_h),
            (new_emb, new_emb_h), (next_attn, next_attn_h), (next_in, next_in_h), (next_out, next_out_h),
            (next_small, next_small_h), (next_emb, next_emb_h),
        ))
    ]

    bar = pltpu.get_barrier_semaphore()

    @pl.loop(1, F)
    def _(d):
        pl.semaphore_signal(bar, inc=1, device_id={"fsdp": peer_f(d)}, device_id_type=pl.DeviceIdType.MESH)

    @pl.loop(1, G)
    def _(d):
        pl.semaphore_signal(bar, inc=1, device_id={"rep": peer_g(d)}, device_id_type=pl.DeviceIdType.MESH)

    def near(n):
        return {"tp": tp - x + lax.rem(x + n // 2, 4), "fsdp": f if n % 2 == 0 else f + 1 - 2 * c}

    for n in range(2, 8):
        pl.semaphore_signal(bar, inc=1, device_id=near(n), device_id_type=pl.DeviceIdType.MESH)

    for load in loads[:2]:
        load.wait()
    for q in range(G):
        for h in range(8):
            rts_own[q, h, :, 0:192] = right[h * 8 : (h + 1) * 8, q * 192 : (q + 1) * 192]
    rts[part, g] = rts_own[g, part]

    pl.semaphore_wait(bar, F + G + 4)

    def rep_copy(src, dst, ss, rs, d):
        return pltpu.make_async_remote_copy(
            src_ref=src, dst_ref=dst, send_sem=ss.at[d], recv_sem=rs.at[d],
            device_id={"rep": peer_g(d)}, device_id_type=pl.DeviceIdType.MESH)

    def right_copy(d):
        return rep_copy(rts_own.at[peer_g(d), part], rts.at[part, g], r_ss, r_rs, d)

    def line(blocks, up_ss, down_ss, rs):
        def hop(k, step):
            ss = up_ss if step > 0 else down_ss
            return pltpu.make_async_remote_copy(
                src_ref=blocks.at[k], dst_ref=blocks.at[k], send_sem=ss.at[k], recv_sem=rs.at[k],
                device_id={"rep": jnp.clip(g + step, 0, G - 1)}, device_id_type=pl.DeviceIdType.MESH)

        def own():
            @pl.when(g < G - 1)
            def _():
                hop(g, 1).start()

            @pl.when(g > 0)
            def _():
                hop(g, -1).start()

        def pass_on(d):
            low = jnp.maximum(g - d, 0)
            high = jnp.minimum(g + d, G - 1)

            @pl.when(g >= d)
            def _():
                hop(low, 1).wait_recv()

                @pl.when(g < G - 1)
                def _():
                    hop(low, 1).start()

            @pl.when(g + d < G)
            def _():
                hop(high, -1).wait_recv()

                @pl.when(g > 0)
                def _():
                    hop(high, -1).start()

        def wait_send():
            @pl.loop(0, G)
            def _(k):
                @pl.when(jnp.logical_and(k <= g, g < G - 1))
                def _():
                    hop(k, 1).wait_send()

                @pl.when(jnp.logical_and(k >= g, g > 0))
                def _():
                    hop(k, -1).wait_send()

        return own, pass_on, wait_send

    left_own, left_pass, left_wait_send = line(lts, lu_ss, ld_ss, l_rs)
    sums_own, sums_pass, sums_wait_send = line(sums, su_ss, sd_ss, s_rs)

    def quarter_copy(d):
        return rep_copy(quart.at[peer_g(d)], quart_in.at[g], q_ss, q_rs, d)

    def near_copy(n):
        return pltpu.make_async_remote_copy(
            src_ref=rts.at[part], dst_ref=rts.at[part], send_sem=x_ss.at[n], recv_sem=x_rs.at[n],
            device_id=near(n), device_id_type=pl.DeviceIdType.MESH)

    def anchor_copy(d):
        return pltpu.make_async_remote_copy(
            src_ref=amsg.at[peer_f(d)], dst_ref=arecv.at[f], send_sem=a_ss.at[d], recv_sem=a_rs.at[d],
            device_id={"fsdp": peer_f(d)}, device_id_type=pl.DeviceIdType.MESH)

    def total_copy(d):
        return pltpu.make_async_remote_copy(
            src_ref=umsg.at[peer_f(d)], dst_ref=urecv.at[f], send_sem=u_ss.at[d], recv_sem=u_rs.at[d],
            device_id={"fsdp": peer_f(d)}, device_id_type=pl.DeviceIdType.MESH)

    def each(copy, n, what):
        @pl.loop(1, n)
        def _(d):
            getattr(copy(d), what)()

    each(right_copy, G, "start")
    left_own()

    for load in loads[2:6]:
        load.wait()

    for t in range(F):
        quart[0, 112 + t : 113 + t, 0:120] = d_small[:, t * 120 : (t + 1) * 120]
    small = quart[0, 112:128, 0:120]
    x_in = d_in[...]
    for q in range(G):
        x_q = dot(x_in, pick_columns(q), 1, 0)
        quart[q, 0:48, 0:96] = d_attn[q * 48 : (q + 1) * 48, :]
        quart[q, 0:48, 96:128] = x_q[:, 0:32]
        quart[q, 48:96, 0:96] = d_out[q * 48 : (q + 1) * 48, :]
        quart[q, 48:96, 96:128] = x_q[:, 32:64]
        for b in range(3):
            quart[q, 96:112, b * 32 : (b + 1) * 32] = x_q[b * 16 : (b + 1) * 16, 64:96]
        if q:
            quart[q, 112:128, 0:120] = small
    quart_in[g] = quart[g]

    left_pass(1)
    each(right_copy, G, "wait_recv")
    for n in range(1, 8):
        near_copy(n).start()
    each(quarter_copy, G, "start")

    for load in loads[6:]:
        load.wait()

    @pl.loop(0, 125, unroll=5)
    def _(p):
        at = pl.ds(pl.multiple_of(p * 384, 128), 384)
        x = a_emb[:, at] - KEEP * m_emb[:, at]
        base[pl.ds(2 * p, 1), 0:192] = x[:, 0:192]
        base[pl.ds(2 * p + 1, 1), 0:192] = x[:, 192:384]

    base[250:251, 0:192] = a_emb[:, 48000:48192] - KEEP * m_emb[:, 48000:48192]

    left_pass(2)

    amsg[...] = jnp.zeros((F, 8, 640), jnp.float32)
    lin[0] = a_attn[...] - KEEP * m_attn[...]
    lin[1] = a_out[...] - KEEP * m_out[...]
    lin[2] = a_in[...] - KEEP * m_in[...]
    for q in range(G):
        for s in range(6):
            wide[q, 0:6, s * 128 : (s + 1) * 128] = lin[0, pl.ds(q * 6 + s, 6, stride=24), :]
            wide[4 + q, 0:6, s * 128 : (s + 1) * 128] = lin[2, pl.ds(q * 36 + s, 6, stride=6), :]
    for s in range(24):
        widef[0:6, s * 128 : (s + 1) * 128] = lin[1, pl.ds(s, 6, stride=24), :]
    share = a_small[...] - KEEP * m_small[...]
    for t in range(F):
        for q in range(G):
            amsg[t, 0:6, q * 144 : q * 144 + 48] = wide[q, 0:6, t * 48 : (t + 1) * 48]
            amsg[t, 0:6, q * 144 + 48 : q * 144 + 96] = widef[0:6, t * 192 + q * 48 : t * 192 + q * 48 + 48]
            amsg[t, 0:6, q * 144 + 96 : q * 144 + 144] = wide[4 + q, 0:6, t * 48 : (t + 1) * 48]
        amsg[t, 6:7, 0:120] = share
    arecv[f] = amsg[f]
    each(anchor_copy, F, "start")

    left_pass(3)
    for n in range(1, 8):
        near_copy(n).wait_recv()
    rhs = jnp.concatenate([rts[:, k, :, :].reshape(64, 256) for k in range(G)], axis=0)
    u_emb = dot(lts[...].reshape(256, ROWS), rhs[:, 0:192], 0, 0)
    un[0:ROWS, 0:192] = u_emb
    base[0:ROWS, 0:192] = base[0:ROWS, 0:192] - STEP * u_emb
    et[...] = jnp.transpose(base[...])[0:192, 0:ROWS].reshape(4, 48, ROWS)

    def emb_copy(i):
        return pltpu.make_async_remote_copy(
            src_ref=et.at[i], dst_ref=gath.at[f], send_sem=e_ss.at[i], recv_sem=e_rs.at[f],
            device_id={"fsdp": g * 4 + i}, device_id_type=pl.DeviceIdType.MESH)

    plane = lax.div(f, 4)

    @pl.loop(0, 4)
    def _(i):
        @pl.when(f != g * 4 + i)
        def _():
            emb_copy(i).start()

    @pl.when(plane == g)
    def _():
        gath[f] = et[lax.rem(f, 4)]

    each(quarter_copy, G, "wait_recv")
    own_sum[...] = quart_in[0] + quart_in[1] + quart_in[2] + quart_in[3]
    sums[g] = own_sum[0:112, :]
    sums_own()

    @pl.loop(0, 125, unroll=5)
    def _(p):
        at = pl.ds(pl.multiple_of(p * 384, 128), 384)
        x = jnp.concatenate([un[pl.ds(2 * p, 1), 0:192], un[pl.ds(2 * p + 1, 1), 0:192]], axis=1)
        next_emb[:, at] = MOMENTUM_COEF * m_emb[:, at] + MEAN * x

    next_emb[:, 48000:48192] = MOMENTUM_COEF * m_emb[:, 48000:48192] + MEAN * un[250:251, 0:192]
    stores[9].start()

    for d in range(1, G):
        sums_pass(d)
    for q in range(G):
        tot[q, 0:96, 0:96] = sums[q, 0:96, 0:96]
        tot[q, 96:144, 0:32] = sums[q, 0:48, 96:128]
        tot[q, 96:144, 32:64] = sums[q, 48:96, 96:128]
        for b in range(3):
            tot[q, 96 + b * 16 : 112 + b * 16, 64:96] = sums[q, 96:112, b * 32 : (b + 1) * 32]
    total = tot[...].reshape(576, 128)[:, 0:96]
    spread = spread_rows()
    umsg[:, :, 0:576] = dot(spread, total, 1, 1).reshape(F, 8, 576)
    urecv[f] = umsg[f]
    each(total_copy, F, "start")

    up = jnp.logical_and(g >= plane, g < G - 1)
    down = jnp.logical_and(g <= plane, g > 0)

    def up_copy(s):
        return pltpu.make_async_remote_copy(
            src_ref=gath.at[s], dst_ref=gath.at[s], send_sem=up_ss.at[s], recv_sem=e_rs.at[s],
            device_id={"rep": jnp.minimum(g + 1, G - 1)}, device_id_type=pl.DeviceIdType.MESH)

    def down_copy(s):
        return pltpu.make_async_remote_copy(
            src_ref=gath.at[s], dst_ref=gath.at[s], send_sem=dn_ss.at[s], recv_sem=e_rs.at[s],
            device_id={"rep": jnp.maximum(g - 1, 0)}, device_id_type=pl.DeviceIdType.MESH)

    def relay(lo, hi):
        @pl.loop(lo, hi)
        def _(k):
            s = peer_f(k)

            @pl.when(jnp.logical_or(plane != g, s != f))
            def _():
                up_copy(s).wait_recv()

            @pl.when(up)
            def _():
                up_copy(s).start()

            @pl.when(down)
            def _():
                down_copy(s).start()

    relay(0, 6)

    each(anchor_copy, F, "wait_recv")
    fixed = dot(arecv[...].reshape(128, 640)[:, 0:576], spread, 0, 0)
    fresh = fixed - STEP * total
    acc = jnp.zeros((48, 384), jnp.float32)
    for q in range(G):
        new_attn[q * 48 : (q + 1) * 48, :] = fresh[q * 144 : q * 144 + 48, :]
        new_out[q * 48 : (q + 1) * 48, :] = fresh[q * 144 + 48 : q * 144 + 96, :]
        acc = acc + dot(fresh[q * 144 + 96 : q * 144 + 144, :], pick_columns(q), 1, 1)
    new_in[...] = acc
    for t in range(F):
        flat_small[:, t * 120 : (t + 1) * 120] = arecv[t, 6:7, 0:120] - STEP * own_sum[112 + t : 113 + t, 0:120]
    for t in range(15):
        new_small[t : t + 1, :] = flat_small[:, t * 128 : (t + 1) * 128]
    next_small[...] = MOMENTUM_COEF * m_small[...] + MEAN * own_sum[pl.ds(112 + f, 1), 0:120]
    for i in (0, 1, 2, 3, 8):
        stores[i].start()

    relay(6, 11)

    each(total_copy, F, "wait_recv")
    for t in range(F):
        for q in range(G):
            wide[q, :, t * 48 : (t + 1) * 48] = urecv[t, :, q * 144 : q * 144 + 48]
            widef[:, t * 192 + q * 48 : t * 192 + q * 48 + 48] = urecv[t, :, q * 144 + 48 : q * 144 + 96]
            wide[4 + q, :, t * 48 : (t + 1) * 48] = urecv[t, :, q * 144 + 96 : q * 144 + 144]
    for q in range(G):
        for s in range(6):
            lin[0, pl.ds(q * 6 + s, 6, stride=24), :] = wide[q, 0:6, s * 128 : (s + 1) * 128]
            lin[2, pl.ds(q * 36 + s, 6, stride=6), :] = wide[4 + q, 0:6, s * 128 : (s + 1) * 128]
    for s in range(24):
        lin[1, pl.ds(s, 6, stride=24), :] = widef[0:6, s * 128 : (s + 1) * 128]
    next_attn[...] = MOMENTUM_COEF * m_attn[...] + MEAN * lin[0]
    next_out[...] = MOMENTUM_COEF * m_out[...] + MEAN * lin[1]
    next_in[...] = MOMENTUM_COEF * m_in[...] + MEAN * lin[2]
    for i in (5, 6, 7):
        stores[i].start()

    relay(11, F)
    for s in range(F):
        new_emb[:, s * ROWS : (s + 1) * ROWS] = gath[s]
    stores[4].start()

    left_wait_send()
    each(right_copy, G, "wait_send")
    for n in range(1, 8):
        near_copy(n).wait_send()
    each(quarter_copy, G, "wait_send")
    sums_wait_send()
    each(anchor_copy, F, "wait_send")
    each(total_copy, F, "wait_send")

    @pl.loop(0, 4)
    def _(i):
        @pl.when(f != g * 4 + i)
        def _():
            emb_copy(i).wait_send()

    @pl.loop(0, F)
    def _(s):
        @pl.when(up)
        def _():
            up_copy(s).wait_send()

        @pl.when(down)
        def _():
            down_copy(s).wait_send()

    for store in stores:
        store.wait()


def write_out(*refs):
    n = (len(refs) - 2) // 3
    took, gave = refs[3 * n], refs[3 * n + 1]
    inward = [pltpu.make_async_copy(refs[i], refs[2 * n + i], took.at[i]) for i in range(n)]
    outward = [pltpu.make_async_copy(refs[2 * n + i], refs[n + i], gave.at[i]) for i in range(n)]
    for copy in inward:
        copy.start()
    for i in range(n):
        inward[i].wait()
        outward[i].start()
    for copy in outward:
        copy.wait()


def on_device(
    delta_attn, delta_in, delta_out, delta_small, emb_left, emb_right,
    anchor_attn, anchor_in, anchor_out, anchor_small, anchor_emb,
    moment_attn, moment_in, moment_out, moment_small, moment_emb,
):
    f32 = jnp.float32
    shape = lambda *s: jax.ShapeDtypeStruct(s, f32)
    hbm = pl.BlockSpec(memory_space=pltpu.HBM)
    buf = lambda *s: pltpu.VMEM(s, f32)
    sem = lambda n: pltpu.SemaphoreType.DMA((n,))
    results = (
        shape(192, 96), shape(48, 384), shape(192, 96), shape(15, 128), shape(48, 4016),
        shape(144, 128), shape(144, 128), shape(144, 128), shape(1, 120), shape(1, 48192),
    )
    held = pl.pallas_call(
        kernel,
        out_shape=results,
        in_specs=[hbm] * 16,
        out_specs=(hbm,) * 10,
        scratch_shapes=[
            *(pltpu.VMEM(r.shape, f32) for r in results),
            buf(192, 96), buf(48, 384), buf(192, 96), buf(1, 1920), buf(64, 768),
            buf(144, 128), buf(144, 128), buf(144, 128), buf(1, 120), buf(1, 48192),
            buf(144, 128), buf(144, 128), buf(144, 128), buf(1, 120), buf(1, 48192),
            buf(1, 1920), buf(3, 144, 128), buf(8, 8, 768), buf(8, 3072),
            buf(4, 128, 128), buf(4, 128, 128), buf(128, 128), buf(4, 112, 128), buf(4, 144, 128),
            buf(4, 64, ROWS), buf(4, 8, 8, 256), buf(8, 4, 8, 256),
            buf(256, 256), buf(256, 256), buf(4, 48, ROWS),
            buf(F, 8, 640), buf(F, 8, 640), buf(F, 8, 640), buf(F, 8, 640), buf(F, 48, ROWS),
            sem(16), sem(10), sem(G), sem(G), sem(G), sem(G), sem(G), sem(G), sem(G), sem(8), sem(8), sem(F), sem(F), sem(G), sem(G), sem(G),
            sem(F), sem(F), sem(4), sem(F), sem(F), sem(F),
        ],
        compiler_params=pltpu.CompilerParams(collective_id=0, has_side_effects=True, vmem_limit_bytes=60 * 2**20),
        name="outer_step",
    )(
        delta_attn.reshape(192, 96), delta_in[0], delta_out[0], delta_small, emb_left[0, 0].T, emb_right[0],
        anchor_attn.reshape(144, 128), anchor_in.reshape(144, 128), anchor_out.reshape(144, 128),
        anchor_small.reshape(1, 120), anchor_emb.reshape(1, 48192),
        moment_attn.reshape(144, 128), moment_in.reshape(144, 128), moment_out.reshape(144, 128),
        moment_small.reshape(1, 120), moment_emb.reshape(1, 48192),
    )
    outs = pl.pallas_call(
        write_out,
        out_shape=results,
        in_specs=[hbm] * 10,
        out_specs=(hbm,) * 10,
        scratch_shapes=[*(pltpu.VMEM(r.shape, f32) for r in results), sem(10), sem(10)],
        compiler_params=pltpu.CompilerParams(vmem_limit_bytes=60 * 2**20),
        name="write_out",
    )(*held)
    return (
        outs[0].reshape(4, 48, 96), outs[1], outs[2], outs[3].reshape(1920), outs[4].T,
        outs[5].reshape(1, 18432), outs[6].reshape(1, 18432), outs[7].reshape(1, 18432),
        outs[8].reshape(120), outs[9].reshape(1, 1, 1, 48192),
    )


def solution(mesh):
    placed = (
        P("rep", None, "fsdp", "tp"),
        P("rep", "fsdp", "tp"),
        P("rep", "fsdp", "tp"),
        P("rep", None),
        P("rep", "tp", "fsdp", None),
        P("rep", None, None),
        P("tp", "fsdp"),
        P("tp", "fsdp"),
        P("tp", "fsdp"),
        P("fsdp"),
        P("tp", "fsdp", "rep", None),
        P("tp", "fsdp"),
        P("tp", "fsdp"),
        P("tp", "fsdp"),
        P("fsdp"),
        P("tp", "fsdp", "rep", None),
    )
    return jax.shard_map(
        on_device,
        mesh=mesh,
        in_specs=placed,
        out_specs=(
            P(None, "fsdp", "tp"),
            P("fsdp", "tp"),
            P("fsdp", "tp"),
            P(),
            P("tp", "fsdp"),
            P("tp", "fsdp"),
            P("tp", "fsdp"),
            P("tp", "fsdp"),
            P("fsdp"),
            P("tp", "fsdp", "rep", None),
        ),
        check_vma=False,
    )
```

```python
import jax
import jax.numpy as jnp
from jax import lax
from jax.experimental import pallas as pl
from jax.experimental.pallas import tpu as pltpu
from jax.sharding import PartitionSpec as P

OUTER_RATE = 0.7
MOMENTUM_COEF = 0.9
G = 4
F = 16
ROWS = 251
KEEP = OUTER_RATE * MOMENTUM_COEF * MOMENTUM_COEF
STEP = OUTER_RATE * (1.0 + MOMENTUM_COEF) / G
MEAN = 1.0 / G


def dot(a, b, ca, cb):
    return lax.dot_general(
        a, b, (((ca,), (cb,)), ((), ())), precision=lax.Precision.HIGHEST, preferred_element_type=jnp.float32
    )


def sixth(d):
    return (d * 43) >> 8


def spread_rows():
    row = lax.broadcasted_iota(jnp.int32, (128, 96), 0)
    col = lax.broadcasted_iota(jnp.int32, (128, 96), 1)
    return (row == col + 2 * sixth(col)).astype(jnp.float32)


def pick_columns(q):
    row = lax.broadcasted_iota(jnp.int32, (384, 96), 0)
    col = lax.broadcasted_iota(jnp.int32, (384, 96), 1)
    return (row == col + 18 * sixth(col) + 6 * q).astype(jnp.float32)


def kernel(
    d_attn_h, d_in_h, d_out_h, d_small_h, left_h, right_h,
    a_attn_h, a_in_h, a_out_h, a_small_h, a_emb_h,
    m_attn_h, m_in_h, m_out_h, m_small_h, m_emb_h,
    new_attn_h, new_in_h, new_out_h, new_small_h, new_emb_h,
    next_attn_h, next_in_h, next_out_h, next_small_h, next_emb_h,
    new_attn, new_in, new_out, new_small, new_emb,
    next_attn, next_in, next_out, next_small, next_emb,
    d_attn, d_in, d_out, d_small, right,
    a_attn, a_in, a_out, a_small, a_emb,
    m_attn, m_in, m_out, m_small, m_emb,
    flat_small, lin, wide, widef, quart, quart_in, own_sum, sums, tot, lts, rts_own, rts, base, un, et,
    amsg, arecv, umsg, urecv, gath,
    in_s, out_s, q_ss, q_rs, l_ss, l_rs, r_ss, r_rs, x_ss, x_rs, a_ss, a_rs, s_ss, s_rs, u_ss, u_rs, e_ss, up_ss, dn_ss, e_rs,
):
    f = lax.axis_index("fsdp")
    g = lax.axis_index("rep")
    c = lax.rem(f, 2)

    def peer_f(d):
        return lax.rem(f + d, F)

    def peer_g(d):
        return lax.rem(g + d, G)

    loads = [
        pltpu.make_async_copy(src, dst, in_s.at[i])
        for i, (src, dst) in enumerate((
            (left_h, lts.at[g]), (right_h, right), (d_in_h, d_in), (d_attn_h, d_attn), (d_out_h, d_out),
            (d_small_h, d_small), (a_attn_h, a_attn), (m_attn_h, m_attn), (a_out_h, a_out), (m_out_h, m_out),
            (a_in_h, a_in), (m_in_h, m_in), (a_small_h, a_small), (m_small_h, m_small), (a_emb_h, a_emb),
            (m_emb_h, m_emb),
        ))
    ]
    for load in loads:
        load.start()
    stores = [
        pltpu.make_async_copy(src, dst, out_s.at[i])
        for i, (src, dst) in enumerate((
            (new_attn, new_attn_h), (new_in, new_in_h), (new_out, new_out_h), (new_small, new_small_h),
            (new_emb, new_emb_h), (next_attn, next_attn_h), (next_in, next_in_h), (next_out, next_out_h),
            (next_small, next_small_h), (next_emb, next_emb_h),
        ))
    ]

    bar = pltpu.get_barrier_semaphore()

    @pl.loop(1, F)
    def _(d):
        pl.semaphore_signal(bar, inc=1, device_id={"fsdp": peer_f(d)}, device_id_type=pl.DeviceIdType.MESH)

    @pl.loop(1, G)
    def _(d):
        pl.semaphore_signal(bar, inc=1, device_id={"rep": peer_g(d)}, device_id_type=pl.DeviceIdType.MESH)

    for load in loads[:2]:
        load.wait()
    for q in range(G):
        for h in range(2):
            rts_own[q, h, :, 0:192] = right[h * 32 : (h + 1) * 32, q * 192 : (q + 1) * 192]
    rts[g] = rts_own[g]

    pl.semaphore_wait(bar, F + G - 2)

    def rep_copy(src, dst, ss, rs, d):
        return pltpu.make_async_remote_copy(
            src_ref=src, dst_ref=dst, send_sem=ss.at[d], recv_sem=rs.at[d],
            device_id={"rep": peer_g(d)}, device_id_type=pl.DeviceIdType.MESH)

    def left_copy(d):
        return rep_copy(lts.at[g], lts.at[g], l_ss, l_rs, d)

    def right_copy(d):
        return rep_copy(rts_own.at[peer_g(d), c], rts.at[g, c], r_ss, r_rs, d)

    def quarter_copy(d):
        return rep_copy(quart.at[peer_g(d)], quart_in.at[g], q_ss, q_rs, d)

    def sum_copy(d):
        return rep_copy(own_sum.at[pl.ds(0, 112)], sums.at[g], s_ss, s_rs, d)

    def half_copy(d):
        part = rts.at[peer_g(G - d), c]
        return pltpu.make_async_remote_copy(
            src_ref=part, dst_ref=part, send_sem=x_ss.at[d], recv_sem=x_rs.at[d],
            device_id={"fsdp": f + 1 - 2 * c}, device_id_type=pl.DeviceIdType.MESH)

    def anchor_copy(d):
        return pltpu.make_async_remote_copy(
            src_ref=amsg.at[peer_f(d)], dst_ref=arecv.at[f], send_sem=a_ss.at[d], recv_sem=a_rs.at[d],
            device_id={"fsdp": peer_f(d)}, device_id_type=pl.DeviceIdType.MESH)

    def total_copy(d):
        return pltpu.make_async_remote_copy(
            src_ref=umsg.at[peer_f(d)], dst_ref=urecv.at[f], send_sem=u_ss.at[d], recv_sem=u_rs.at[d],
            device_id={"fsdp": peer_f(d)}, device_id_type=pl.DeviceIdType.MESH)

    def each(copy, n, what):
        @pl.loop(1, n)
        def _(d):
            getattr(copy(d), what)()

    each(right_copy, G, "start")
    each(left_copy, G, "start")

    for load in loads[2:6]:
        load.wait()

    for t in range(F):
        quart[0, 112 + t : 113 + t, 0:120] = d_small[:, t * 120 : (t + 1) * 120]
    small = quart[0, 112:128, 0:120]
    x_in = d_in[...]
    for q in range(G):
        x_q = dot(x_in, pick_columns(q), 1, 0)
        quart[q, 0:48, 0:96] = d_attn[q * 48 : (q + 1) * 48, :]
        quart[q, 0:48, 96:128] = x_q[:, 0:32]
        quart[q, 48:96, 0:96] = d_out[q * 48 : (q + 1) * 48, :]
        quart[q, 48:96, 96:128] = x_q[:, 32:64]
        for b in range(3):
            quart[q, 96:112, b * 32 : (b + 1) * 32] = x_q[b * 16 : (b + 1) * 16, 64:96]
        if q:
            quart[q, 112:128, 0:120] = small
    quart_in[g] = quart[g]

    @pl.loop(1, G)
    def _(d):
        right_copy(d).wait_recv()
        half_copy(d).start()

    each(quarter_copy, G, "start")

    for load in loads[6:]:
        load.wait()

    @pl.loop(0, 125, unroll=5)
    def _(p):
        at = pl.ds(pl.multiple_of(p * 384, 128), 384)
        x = a_emb[:, at] - KEEP * m_emb[:, at]
        base[pl.ds(2 * p, 1), 0:192] = x[:, 0:192]
        base[pl.ds(2 * p + 1, 1), 0:192] = x[:, 192:384]

    base[250:251, 0:192] = a_emb[:, 48000:48192] - KEEP * m_emb[:, 48000:48192]

    amsg[...] = jnp.zeros((F, 8, 640), jnp.float32)
    lin[0] = a_attn[...] - KEEP * m_attn[...]
    lin[1] = a_out[...] - KEEP * m_out[...]
    lin[2] = a_in[...] - KEEP * m_in[...]
    for q in range(G):
        for s in range(6):
            wide[q, 0:6, s * 128 : (s + 1) * 128] = lin[0, pl.ds(q * 6 + s, 6, stride=24), :]
            wide[4 + q, 0:6, s * 128 : (s + 1) * 128] = lin[2, pl.ds(q * 36 + s, 6, stride=6), :]
    for s in range(24):
        widef[0:6, s * 128 : (s + 1) * 128] = lin[1, pl.ds(s, 6, stride=24), :]
    share = a_small[...] - KEEP * m_small[...]
    for t in range(F):
        for q in range(G):
            amsg[t, 0:6, q * 144 : q * 144 + 48] = wide[q, 0:6, t * 48 : (t + 1) * 48]
            amsg[t, 0:6, q * 144 + 48 : q * 144 + 96] = widef[0:6, t * 192 + q * 48 : t * 192 + q * 48 + 48]
            amsg[t, 0:6, q * 144 + 96 : q * 144 + 144] = wide[4 + q, 0:6, t * 48 : (t + 1) * 48]
        amsg[t, 6:7, 0:120] = share
    arecv[f] = amsg[f]
    each(anchor_copy, F, "start")

    each(left_copy, G, "wait_recv")
    each(half_copy, G, "wait_recv")
    u_emb = dot(lts[...].reshape(256, ROWS), rts[...].reshape(256, 256)[:, 0:192], 0, 0)
    un[0:ROWS, 0:192] = u_emb
    base[0:ROWS, 0:192] = base[0:ROWS, 0:192] - STEP * u_emb
    et[...] = jnp.transpose(base[...])[0:192, 0:ROWS].reshape(4, 48, ROWS)

    def emb_copy(i):
        return pltpu.make_async_remote_copy(
            src_ref=et.at[i], dst_ref=gath.at[f], send_sem=e_ss.at[i], recv_sem=e_rs.at[f],
            device_id={"fsdp": g * 4 + i}, device_id_type=pl.DeviceIdType.MESH)

    plane = lax.div(f, 4)

    @pl.loop(0, 4)
    def _(i):
        @pl.when(f != g * 4 + i)
        def _():
            emb_copy(i).start()

    @pl.when(plane == g)
    def _():
        gath[f] = et[lax.rem(f, 4)]

    each(quarter_copy, G, "wait_recv")
    own_sum[...] = quart_in[0] + quart_in[1] + quart_in[2] + quart_in[3]
    sums[g] = own_sum[0:112, :]
    each(sum_copy, G, "start")

    up = jnp.logical_and(g >= plane, g < G - 1)
    down = jnp.logical_and(g <= plane, g > 0)

    def up_copy(s):
        return pltpu.make_async_remote_copy(
            src_ref=gath.at[s], dst_ref=gath.at[s], send_sem=up_ss.at[s], recv_sem=e_rs.at[s],
            device_id={"rep": jnp.minimum(g + 1, G - 1)}, device_id_type=pl.DeviceIdType.MESH)

    def down_copy(s):
        return pltpu.make_async_remote_copy(
            src_ref=gath.at[s], dst_ref=gath.at[s], send_sem=dn_ss.at[s], recv_sem=e_rs.at[s],
            device_id={"rep": jnp.maximum(g - 1, 0)}, device_id_type=pl.DeviceIdType.MESH)

    def relay(lo, hi):
        @pl.loop(lo, hi)
        def _(k):
            off = lax.div(k + 1, 2)
            s = peer_f(jnp.where(lax.rem(k, 2) == 1, off, F - off))

            @pl.when(jnp.logical_or(plane != g, s != f))
            def _():
                up_copy(s).wait_recv()

            @pl.when(up)
            def _():
                up_copy(s).start()

            @pl.when(down)
            def _():
                down_copy(s).start()

    relay(0, 4)

    each(sum_copy, G, "wait_recv")
    for q in range(G):
        tot[q, 0:96, 0:96] = sums[q, 0:96, 0:96]
        tot[q, 96:144, 0:32] = sums[q, 0:48, 96:128]
        tot[q, 96:144, 32:64] = sums[q, 48:96, 96:128]
        for b in range(3):
            tot[q, 96 + b * 16 : 112 + b * 16, 64:96] = sums[q, 96:112, b * 32 : (b + 1) * 32]
    total = tot[...].reshape(576, 128)[:, 0:96]
    spread = spread_rows()
    umsg[:, :, 0:576] = dot(spread, total, 1, 1).reshape(F, 8, 576)
    urecv[f] = umsg[f]
    each(total_copy, F, "start")

    relay(4, 9)

    each(anchor_copy, F, "wait_recv")
    fixed = dot(arecv[...].reshape(128, 640)[:, 0:576], spread, 0, 0)
    fresh = fixed - STEP * total
    acc = jnp.zeros((48, 384), jnp.float32)
    for q in range(G):
        new_attn[q * 48 : (q + 1) * 48, :] = fresh[q * 144 : q * 144 + 48, :]
        new_out[q * 48 : (q + 1) * 48, :] = fresh[q * 144 + 48 : q * 144 + 96, :]
        acc = acc + dot(fresh[q * 144 + 96 : q * 144 + 144, :], pick_columns(q), 1, 1)
    new_in[...] = acc
    for t in range(F):
        flat_small[:, t * 120 : (t + 1) * 120] = arecv[t, 6:7, 0:120] - STEP * own_sum[112 + t : 113 + t, 0:120]
    for t in range(15):
        new_small[t : t + 1, :] = flat_small[:, t * 128 : (t + 1) * 128]
    next_small[...] = MOMENTUM_COEF * m_small[...] + MEAN * own_sum[pl.ds(112 + f, 1), 0:120]
    for i in (0, 1, 2, 3, 8):
        stores[i].start()

    relay(9, 13)

    @pl.loop(0, 125, unroll=5)
    def _(p):
        at = pl.ds(pl.multiple_of(p * 384, 128), 384)
        x = jnp.concatenate([un[pl.ds(2 * p, 1), 0:192], un[pl.ds(2 * p + 1, 1), 0:192]], axis=1)
        next_emb[:, at] = MOMENTUM_COEF * m_emb[:, at] + MEAN * x

    next_emb[:, 48000:48192] = MOMENTUM_COEF * m_emb[:, 48000:48192] + MEAN * un[250:251, 0:192]
    stores[9].start()

    each(total_copy, F, "wait_recv")
    for t in range(F):
        for q in range(G):
            wide[q, :, t * 48 : (t + 1) * 48] = urecv[t, :, q * 144 : q * 144 + 48]
            widef[:, t * 192 + q * 48 : t * 192 + q * 48 + 48] = urecv[t, :, q * 144 + 48 : q * 144 + 96]
            wide[4 + q, :, t * 48 : (t + 1) * 48] = urecv[t, :, q * 144 + 96 : q * 144 + 144]
    for q in range(G):
        for s in range(6):
            lin[0, pl.ds(q * 6 + s, 6, stride=24), :] = wide[q, 0:6, s * 128 : (s + 1) * 128]
            lin[2, pl.ds(q * 36 + s, 6, stride=6), :] = wide[4 + q, 0:6, s * 128 : (s + 1) * 128]
    for s in range(24):
        lin[1, pl.ds(s, 6, stride=24), :] = widef[0:6, s * 128 : (s + 1) * 128]
    next_attn[...] = MOMENTUM_COEF * m_attn[...] + MEAN * lin[0]
    next_out[...] = MOMENTUM_COEF * m_out[...] + MEAN * lin[1]
    next_in[...] = MOMENTUM_COEF * m_in[...] + MEAN * lin[2]
    for i in (5, 6, 7):
        stores[i].start()

    relay(13, F)
    for s in range(F):
        new_emb[:, s * ROWS : (s + 1) * ROWS] = gath[s]
    stores[4].start()

    each(left_copy, G, "wait_send")
    each(right_copy, G, "wait_send")
    each(half_copy, G, "wait_send")
    each(quarter_copy, G, "wait_send")
    each(sum_copy, G, "wait_send")
    each(anchor_copy, F, "wait_send")
    each(total_copy, F, "wait_send")

    @pl.loop(0, 4)
    def _(i):
        @pl.when(f != g * 4 + i)
        def _():
            emb_copy(i).wait_send()

    @pl.loop(0, F)
    def _(s):
        @pl.when(up)
        def _():
            up_copy(s).wait_send()

        @pl.when(down)
        def _():
            down_copy(s).wait_send()

    for store in stores:
        store.wait()


def write_out(*refs):
    n = (len(refs) - 2) // 3
    took, gave = refs[3 * n], refs[3 * n + 1]
    inward = [pltpu.make_async_copy(refs[i], refs[2 * n + i], took.at[i]) for i in range(n)]
    outward = [pltpu.make_async_copy(refs[2 * n + i], refs[n + i], gave.at[i]) for i in range(n)]
    for copy in inward:
        copy.start()
    for i in range(n):
        inward[i].wait()
        outward[i].start()
    for copy in outward:
        copy.wait()


def on_device(
    delta_attn, delta_in, delta_out, delta_small, emb_left, emb_right,
    anchor_attn, anchor_in, anchor_out, anchor_small, anchor_emb,
    moment_attn, moment_in, moment_out, moment_small, moment_emb,
):
    f32 = jnp.float32
    shape = lambda *s: jax.ShapeDtypeStruct(s, f32)
    hbm = pl.BlockSpec(memory_space=pltpu.HBM)
    buf = lambda *s: pltpu.VMEM(s, f32)
    sem = lambda n: pltpu.SemaphoreType.DMA((n,))
    results = (
        shape(192, 96), shape(48, 384), shape(192, 96), shape(15, 128), shape(48, 4016),
        shape(144, 128), shape(144, 128), shape(144, 128), shape(1, 120), shape(1, 48192),
    )
    held = pl.pallas_call(
        kernel,
        out_shape=results,
        in_specs=[hbm] * 16,
        out_specs=(hbm,) * 10,
        scratch_shapes=[
            *(pltpu.VMEM(r.shape, f32) for r in results),
            buf(192, 96), buf(48, 384), buf(192, 96), buf(1, 1920), buf(64, 768),
            buf(144, 128), buf(144, 128), buf(144, 128), buf(1, 120), buf(1, 48192),
            buf(144, 128), buf(144, 128), buf(144, 128), buf(1, 120), buf(1, 48192),
            buf(1, 1920), buf(3, 144, 128), buf(8, 8, 768), buf(8, 3072),
            buf(4, 128, 128), buf(4, 128, 128), buf(128, 128), buf(4, 112, 128), buf(4, 144, 128),
            buf(4, 64, ROWS), buf(4, 2, 32, 256), buf(4, 2, 32, 256),
            buf(256, 256), buf(256, 256), buf(4, 48, ROWS),
            buf(F, 8, 640), buf(F, 8, 640), buf(F, 8, 640), buf(F, 8, 640), buf(F, 48, ROWS),
            sem(16), sem(10), sem(G), sem(G), sem(G), sem(G), sem(G), sem(G), sem(G), sem(G), sem(F), sem(F), sem(G), sem(G),
            sem(F), sem(F), sem(4), sem(F), sem(F), sem(F),
        ],
        compiler_params=pltpu.CompilerParams(collective_id=0, has_side_effects=True, vmem_limit_bytes=60 * 2**20),
        name="outer_step",
    )(
        delta_attn.reshape(192, 96), delta_in[0], delta_out[0], delta_small, emb_left[0, 0].T, emb_right[0],
        anchor_attn.reshape(144, 128), anchor_in.reshape(144, 128), anchor_out.reshape(144, 128),
        anchor_small.reshape(1, 120), anchor_emb.reshape(1, 48192),
        moment_attn.reshape(144, 128), moment_in.reshape(144, 128), moment_out.reshape(144, 128),
        moment_small.reshape(1, 120), moment_emb.reshape(1, 48192),
    )
    outs = pl.pallas_call(
        write_out,
        out_shape=results,
        in_specs=[hbm] * 10,
        out_specs=(hbm,) * 10,
        scratch_shapes=[*(pltpu.VMEM(r.shape, f32) for r in results), sem(10), sem(10)],
        compiler_params=pltpu.CompilerParams(vmem_limit_bytes=60 * 2**20),
        name="write_out",
    )(*held)
    return (
        outs[0].reshape(4, 48, 96), outs[1], outs[2], outs[3].reshape(1920), outs[4].T,
        outs[5].reshape(1, 18432), outs[6].reshape(1, 18432), outs[7].reshape(1, 18432),
        outs[8].reshape(120), outs[9].reshape(1, 1, 1, 48192),
    )


def solution(mesh):
    placed = (
        P("rep", None, "fsdp", "tp"),
        P("rep", "fsdp", "tp"),
        P("rep", "fsdp", "tp"),
        P("rep", None),
        P("rep", "tp", "fsdp", None),
        P("rep", None, None),
        P("tp", "fsdp"),
        P("tp", "fsdp"),
        P("tp", "fsdp"),
        P("fsdp"),
        P("tp", "fsdp", "rep", None),
        P("tp", "fsdp"),
        P("tp", "fsdp"),
        P("tp", "fsdp"),
        P("fsdp"),
        P("tp", "fsdp", "rep", None),
    )
    return jax.shard_map(
        on_device,
        mesh=mesh,
        in_specs=placed,
        out_specs=(
            P(None, "fsdp", "tp"),
            P("fsdp", "tp"),
            P("fsdp", "tp"),
            P(),
            P("tp", "fsdp"),
            P("tp", "fsdp"),
            P("tp", "fsdp"),
            P("tp", "fsdp"),
            P("fsdp"),
            P("tp", "fsdp", "rep", None),
        ),
        check_vma=False,
    )
```

```python
import jax
import jax.numpy as jnp
from jax import lax
from jax.experimental import pallas as pl
from jax.experimental.pallas import tpu as pltpu
from jax.sharding import PartitionSpec as P

OUTER_RATE = 0.7
MOMENTUM_COEF = 0.9
G = 4
F = 16
ROWS = 251
KEEP = OUTER_RATE * MOMENTUM_COEF * MOMENTUM_COEF
STEP = OUTER_RATE * (1.0 + MOMENTUM_COEF) / G
MEAN = 1.0 / G


def dot(a, b, ca, cb):
    return lax.dot_general(
        a, b, (((ca,), (cb,)), ((), ())), precision=lax.Precision.HIGHEST, preferred_element_type=jnp.float32
    )


def sixth(d):
    return (d * 43) >> 8


def spread_rows():
    row = lax.broadcasted_iota(jnp.int32, (128, 96), 0)
    col = lax.broadcasted_iota(jnp.int32, (128, 96), 1)
    return (row == col + 2 * sixth(col)).astype(jnp.float32)


def pick_columns(q):
    row = lax.broadcasted_iota(jnp.int32, (384, 96), 0)
    col = lax.broadcasted_iota(jnp.int32, (384, 96), 1)
    return (row == col + 18 * sixth(col) + 6 * q).astype(jnp.float32)


def kernel(
    d_attn_h, d_in_h, d_out_h, d_small_h, left_h, right_h,
    a_attn_h, a_in_h, a_out_h, a_small_h, a_emb_h,
    m_attn_h, m_in_h, m_out_h, m_small_h, m_emb_h,
    new_attn_h, new_in_h, new_out_h, new_small_h, new_emb_h,
    next_attn_h, next_in_h, next_out_h, next_small_h, next_emb_h,
    new_attn, new_in, new_out, new_small, new_emb,
    next_attn, next_in, next_out, next_small, next_emb,
    d_attn, d_in, d_out, d_small, right,
    a_attn, a_in, a_out, a_small, a_emb,
    m_attn, m_in, m_out, m_small, m_emb,
    flat_small, lin, wide, widef, quart, quart_in, own_sum, sums, tot, lts, rts_own, rts, base, un, et,
    amsg, arecv, umsg, urecv, gath,
    in_s, out_s, q_ss, q_rs, lu_ss, ld_ss, l_rs, r_ss, r_rs, x_ss, x_rs, a_ss, a_rs, su_ss, sd_ss, s_rs, u_ss, u_rs, e_ss, up_ss, dn_ss, e_rs,
):
    f = lax.axis_index("fsdp")
    g = lax.axis_index("rep")
    c = lax.rem(f, 2)

    def peer_f(d):
        return lax.rem(f + d, F)

    def peer_g(d):
        return lax.rem(g + d, G)

    loads = [
        pltpu.make_async_copy(src, dst, in_s.at[i])
        for i, (src, dst) in enumerate((
            (left_h, lts.at[g]), (right_h, right), (d_in_h, d_in), (d_attn_h, d_attn), (d_out_h, d_out),
            (d_small_h, d_small), (a_attn_h, a_attn), (m_attn_h, m_attn), (a_out_h, a_out), (m_out_h, m_out),
            (a_in_h, a_in), (m_in_h, m_in), (a_small_h, a_small), (m_small_h, m_small), (a_emb_h, a_emb),
            (m_emb_h, m_emb),
        ))
    ]
    for load in loads:
        load.start()
    stores = [
        pltpu.make_async_copy(src, dst, out_s.at[i])
        for i, (src, dst) in enumerate((
            (new_attn, new_attn_h), (new_in, new_in_h), (new_out, new_out_h), (new_small, new_small_h),
            (new_emb, new_emb_h), (next_attn, next_attn_h), (next_in, next_in_h), (next_out, next_out_h),
            (next_small, next_small_h), (next_emb, next_emb_h),
        ))
    ]

    bar = pltpu.get_barrier_semaphore()

    @pl.loop(1, F)
    def _(d):
        pl.semaphore_signal(bar, inc=1, device_id={"fsdp": peer_f(d)}, device_id_type=pl.DeviceIdType.MESH)

    @pl.loop(1, G)
    def _(d):
        pl.semaphore_signal(bar, inc=1, device_id={"rep": peer_g(d)}, device_id_type=pl.DeviceIdType.MESH)

    for load in loads[:2]:
        load.wait()
    for q in range(G):
        for h in range(2):
            rts_own[q, h, :, 0:192] = right[h * 32 : (h + 1) * 32, q * 192 : (q + 1) * 192]
    rts[g] = rts_own[g]

    pl.semaphore_wait(bar, F + G - 2)

    def rep_copy(src, dst, ss, rs, d):
        return pltpu.make_async_remote_copy(
            src_ref=src, dst_ref=dst, send_sem=ss.at[d], recv_sem=rs.at[d],
            device_id={"rep": peer_g(d)}, device_id_type=pl.DeviceIdType.MESH)

    def right_copy(d):
        return rep_copy(rts_own.at[peer_g(d), c], rts.at[g, c], r_ss, r_rs, d)

    def line(blocks, up_ss, down_ss, rs):
        def hop(k, step):
            ss = up_ss if step > 0 else down_ss
            return pltpu.make_async_remote_copy(
                src_ref=blocks.at[k], dst_ref=blocks.at[k], send_sem=ss.at[k], recv_sem=rs.at[k],
                device_id={"rep": jnp.clip(g + step, 0, G - 1)}, device_id_type=pl.DeviceIdType.MESH)

        def own():
            @pl.when(g < G - 1)
            def _():
                hop(g, 1).start()

            @pl.when(g > 0)
            def _():
                hop(g, -1).start()

        def pass_on(d):
            low = jnp.maximum(g - d, 0)
            high = jnp.minimum(g + d, G - 1)

            @pl.when(g >= d)
            def _():
                hop(low, 1).wait_recv()

                @pl.when(g < G - 1)
                def _():
                    hop(low, 1).start()

            @pl.when(g + d < G)
            def _():
                hop(high, -1).wait_recv()

                @pl.when(g > 0)
                def _():
                    hop(high, -1).start()

        def wait_send():
            @pl.loop(0, G)
            def _(k):
                @pl.when(jnp.logical_and(k <= g, g < G - 1))
                def _():
                    hop(k, 1).wait_send()

                @pl.when(jnp.logical_and(k >= g, g > 0))
                def _():
                    hop(k, -1).wait_send()

        return own, pass_on, wait_send

    left_own, left_pass, left_wait_send = line(lts, lu_ss, ld_ss, l_rs)
    sums_own, sums_pass, sums_wait_send = line(sums, su_ss, sd_ss, s_rs)

    def quarter_copy(d):
        return rep_copy(quart.at[peer_g(d)], quart_in.at[g], q_ss, q_rs, d)

    def half_copy(d):
        part = rts.at[peer_g(G - d), c]
        return pltpu.make_async_remote_copy(
            src_ref=part, dst_ref=part, send_sem=x_ss.at[d], recv_sem=x_rs.at[d],
            device_id={"fsdp": f + 1 - 2 * c}, device_id_type=pl.DeviceIdType.MESH)

    def anchor_copy(d):
        return pltpu.make_async_remote_copy(
            src_ref=amsg.at[peer_f(d)], dst_ref=arecv.at[f], send_sem=a_ss.at[d], recv_sem=a_rs.at[d],
            device_id={"fsdp": peer_f(d)}, device_id_type=pl.DeviceIdType.MESH)

    def total_copy(d):
        return pltpu.make_async_remote_copy(
            src_ref=umsg.at[peer_f(d)], dst_ref=urecv.at[f], send_sem=u_ss.at[d], recv_sem=u_rs.at[d],
            device_id={"fsdp": peer_f(d)}, device_id_type=pl.DeviceIdType.MESH)

    def each(copy, n, what):
        @pl.loop(1, n)
        def _(d):
            getattr(copy(d), what)()

    each(right_copy, G, "start")
    left_own()

    for load in loads[2:6]:
        load.wait()

    for t in range(F):
        quart[0, 112 + t : 113 + t, 0:120] = d_small[:, t * 120 : (t + 1) * 120]
    small = quart[0, 112:128, 0:120]
    x_in = d_in[...]
    for q in range(G):
        x_q = dot(x_in, pick_columns(q), 1, 0)
        quart[q, 0:48, 0:96] = d_attn[q * 48 : (q + 1) * 48, :]
        quart[q, 0:48, 96:128] = x_q[:, 0:32]
        quart[q, 48:96, 0:96] = d_out[q * 48 : (q + 1) * 48, :]
        quart[q, 48:96, 96:128] = x_q[:, 32:64]
        for b in range(3):
            quart[q, 96:112, b * 32 : (b + 1) * 32] = x_q[b * 16 : (b + 1) * 16, 64:96]
        if q:
            quart[q, 112:128, 0:120] = small
    quart_in[g] = quart[g]

    @pl.loop(1, G)
    def _(d):
        right_copy(d).wait_recv()
        half_copy(d).start()

    left_pass(1)
    each(quarter_copy, G, "start")

    for load in loads[6:]:
        load.wait()

    @pl.loop(0, 125, unroll=5)
    def _(p):
        at = pl.ds(pl.multiple_of(p * 384, 128), 384)
        x = a_emb[:, at] - KEEP * m_emb[:, at]
        base[pl.ds(2 * p, 1), 0:192] = x[:, 0:192]
        base[pl.ds(2 * p + 1, 1), 0:192] = x[:, 192:384]

    base[250:251, 0:192] = a_emb[:, 48000:48192] - KEEP * m_emb[:, 48000:48192]

    left_pass(2)

    amsg[...] = jnp.zeros((F, 8, 640), jnp.float32)
    lin[0] = a_attn[...] - KEEP * m_attn[...]
    lin[1] = a_out[...] - KEEP * m_out[...]
    lin[2] = a_in[...] - KEEP * m_in[...]
    for q in range(G):
        for s in range(6):
            wide[q, 0:6, s * 128 : (s + 1) * 128] = lin[0, pl.ds(q * 6 + s, 6, stride=24), :]
            wide[4 + q, 0:6, s * 128 : (s + 1) * 128] = lin[2, pl.ds(q * 36 + s, 6, stride=6), :]
    for s in range(24):
        widef[0:6, s * 128 : (s + 1) * 128] = lin[1, pl.ds(s, 6, stride=24), :]
    share = a_small[...] - KEEP * m_small[...]
    for t in range(F):
        for q in range(G):
            amsg[t, 0:6, q * 144 : q * 144 + 48] = wide[q, 0:6, t * 48 : (t + 1) * 48]
            amsg[t, 0:6, q * 144 + 48 : q * 144 + 96] = widef[0:6, t * 192 + q * 48 : t * 192 + q * 48 + 48]
            amsg[t, 0:6, q * 144 + 96 : q * 144 + 144] = wide[4 + q, 0:6, t * 48 : (t + 1) * 48]
        amsg[t, 6:7, 0:120] = share
    arecv[f] = amsg[f]
    each(anchor_copy, F, "start")

    left_pass(3)
    each(half_copy, G, "wait_recv")
    u_emb = dot(lts[...].reshape(256, ROWS), rts[...].reshape(256, 256)[:, 0:192], 0, 0)
    un[0:ROWS, 0:192] = u_emb
    base[0:ROWS, 0:192] = base[0:ROWS, 0:192] - STEP * u_emb
    et[...] = jnp.transpose(base[...])[0:192, 0:ROWS].reshape(4, 48, ROWS)

    def emb_copy(i):
        return pltpu.make_async_remote_copy(
            src_ref=et.at[i], dst_ref=gath.at[f], send_sem=e_ss.at[i], recv_sem=e_rs.at[f],
            device_id={"fsdp": g * 4 + i}, device_id_type=pl.DeviceIdType.MESH)

    plane = lax.div(f, 4)

    @pl.loop(0, 4)
    def _(i):
        @pl.when(f != g * 4 + i)
        def _():
            emb_copy(i).start()

    @pl.when(plane == g)
    def _():
        gath[f] = et[lax.rem(f, 4)]

    up = jnp.logical_and(g >= plane, g < G - 1)
    down = jnp.logical_and(g <= plane, g > 0)

    def up_copy(s):
        return pltpu.make_async_remote_copy(
            src_ref=gath.at[s], dst_ref=gath.at[s], send_sem=up_ss.at[s], recv_sem=e_rs.at[s],
            device_id={"rep": jnp.minimum(g + 1, G - 1)}, device_id_type=pl.DeviceIdType.MESH)

    def down_copy(s):
        return pltpu.make_async_remote_copy(
            src_ref=gath.at[s], dst_ref=gath.at[s], send_sem=dn_ss.at[s], recv_sem=e_rs.at[s],
            device_id={"rep": jnp.maximum(g - 1, 0)}, device_id_type=pl.DeviceIdType.MESH)

    def relay(lo, hi):
        @pl.loop(lo, hi)
        def _(k):
            off = lax.div(k + 1, 2)
            s = peer_f(jnp.where(lax.rem(k, 2) == 1, off, F - off))

            @pl.when(jnp.logical_or(plane != g, s != f))
            def _():
                up_copy(s).wait_recv()

            @pl.when(up)
            def _():
                up_copy(s).start()

            @pl.when(down)
            def _():
                down_copy(s).start()

    relay(0, 2)

    each(quarter_copy, G, "wait_recv")
    own_sum[...] = quart_in[0] + quart_in[1] + quart_in[2] + quart_in[3]
    sums[g] = own_sum[0:112, :]
    sums_own()

    @pl.loop(0, 125, unroll=5)
    def _(p):
        at = pl.ds(pl.multiple_of(p * 384, 128), 384)
        x = jnp.concatenate([un[pl.ds(2 * p, 1), 0:192], un[pl.ds(2 * p + 1, 1), 0:192]], axis=1)
        next_emb[:, at] = MOMENTUM_COEF * m_emb[:, at] + MEAN * x

    next_emb[:, 48000:48192] = MOMENTUM_COEF * m_emb[:, 48000:48192] + MEAN * un[250:251, 0:192]
    stores[9].start()

    relay(2, 6)
    sums_pass(1)
    relay(6, 8)
    sums_pass(2)
    relay(8, 10)
    sums_pass(3)
    for q in range(G):
        tot[q, 0:96, 0:96] = sums[q, 0:96, 0:96]
        tot[q, 96:144, 0:32] = sums[q, 0:48, 96:128]
        tot[q, 96:144, 32:64] = sums[q, 48:96, 96:128]
        for b in range(3):
            tot[q, 96 + b * 16 : 112 + b * 16, 64:96] = sums[q, 96:112, b * 32 : (b + 1) * 32]
    total = tot[...].reshape(576, 128)[:, 0:96]
    spread = spread_rows()
    umsg[:, :, 0:576] = dot(spread, total, 1, 1).reshape(F, 8, 576)
    urecv[f] = umsg[f]
    each(total_copy, F, "start")

    relay(10, 13)

    each(anchor_copy, F, "wait_recv")
    fixed = dot(arecv[...].reshape(128, 640)[:, 0:576], spread, 0, 0)
    fresh = fixed - STEP * total
    acc = jnp.zeros((48, 384), jnp.float32)
    for q in range(G):
        new_attn[q * 48 : (q + 1) * 48, :] = fresh[q * 144 : q * 144 + 48, :]
        new_out[q * 48 : (q + 1) * 48, :] = fresh[q * 144 + 48 : q * 144 + 96, :]
        acc = acc + dot(fresh[q * 144 + 96 : q * 144 + 144, :], pick_columns(q), 1, 1)
    new_in[...] = acc
    for t in range(F):
        flat_small[:, t * 120 : (t + 1) * 120] = arecv[t, 6:7, 0:120] - STEP * own_sum[112 + t : 113 + t, 0:120]
    for t in range(15):
        new_small[t : t + 1, :] = flat_small[:, t * 128 : (t + 1) * 128]
    next_small[...] = MOMENTUM_COEF * m_small[...] + MEAN * own_sum[pl.ds(112 + f, 1), 0:120]
    for i in (0, 1, 2, 3, 8):
        stores[i].start()

    relay(13, F)

    each(total_copy, F, "wait_recv")
    for t in range(F):
        for q in range(G):
            wide[q, :, t * 48 : (t + 1) * 48] = urecv[t, :, q * 144 : q * 144 + 48]
            widef[:, t * 192 + q * 48 : t * 192 + q * 48 + 48] = urecv[t, :, q * 144 + 48 : q * 144 + 96]
            wide[4 + q, :, t * 48 : (t + 1) * 48] = urecv[t, :, q * 144 + 96 : q * 144 + 144]
    for q in range(G):
        for s in range(6):
            lin[0, pl.ds(q * 6 + s, 6, stride=24), :] = wide[q, 0:6, s * 128 : (s + 1) * 128]
            lin[2, pl.ds(q * 36 + s, 6, stride=6), :] = wide[4 + q, 0:6, s * 128 : (s + 1) * 128]
    for s in range(24):
        lin[1, pl.ds(s, 6, stride=24), :] = widef[0:6, s * 128 : (s + 1) * 128]
    next_attn[...] = MOMENTUM_COEF * m_attn[...] + MEAN * lin[0]
    next_out[...] = MOMENTUM_COEF * m_out[...] + MEAN * lin[1]
    next_in[...] = MOMENTUM_COEF * m_in[...] + MEAN * lin[2]
    for i in (5, 6, 7):
        stores[i].start()

    for s in range(F):
        new_emb[:, s * ROWS : (s + 1) * ROWS] = gath[s]
    stores[4].start()

    left_wait_send()
    each(right_copy, G, "wait_send")
    each(half_copy, G, "wait_send")
    each(quarter_copy, G, "wait_send")
    sums_wait_send()
    each(anchor_copy, F, "wait_send")
    each(total_copy, F, "wait_send")

    @pl.loop(0, 4)
    def _(i):
        @pl.when(f != g * 4 + i)
        def _():
            emb_copy(i).wait_send()

    @pl.loop(0, F)
    def _(s):
        @pl.when(up)
        def _():
            up_copy(s).wait_send()

        @pl.when(down)
        def _():
            down_copy(s).wait_send()

    for store in stores:
        store.wait()


def write_out(*refs):
    n = (len(refs) - 2) // 3
    took, gave = refs[3 * n], refs[3 * n + 1]
    inward = [pltpu.make_async_copy(refs[i], refs[2 * n + i], took.at[i]) for i in range(n)]
    outward = [pltpu.make_async_copy(refs[2 * n + i], refs[n + i], gave.at[i]) for i in range(n)]
    for copy in inward:
        copy.start()
    for i in range(n):
        inward[i].wait()
        outward[i].start()
    for copy in outward:
        copy.wait()


def on_device(
    delta_attn, delta_in, delta_out, delta_small, emb_left, emb_right,
    anchor_attn, anchor_in, anchor_out, anchor_small, anchor_emb,
    moment_attn, moment_in, moment_out, moment_small, moment_emb,
):
    f32 = jnp.float32
    shape = lambda *s: jax.ShapeDtypeStruct(s, f32)
    hbm = pl.BlockSpec(memory_space=pltpu.HBM)
    buf = lambda *s: pltpu.VMEM(s, f32)
    sem = lambda n: pltpu.SemaphoreType.DMA((n,))
    results = (
        shape(192, 96), shape(48, 384), shape(192, 96), shape(15, 128), shape(48, 4016),
        shape(144, 128), shape(144, 128), shape(144, 128), shape(1, 120), shape(1, 48192),
    )
    held = pl.pallas_call(
        kernel,
        out_shape=results,
        in_specs=[hbm] * 16,
        out_specs=(hbm,) * 10,
        scratch_shapes=[
            *(pltpu.VMEM(r.shape, f32) for r in results),
            buf(192, 96), buf(48, 384), buf(192, 96), buf(1, 1920), buf(64, 768),
            buf(144, 128), buf(144, 128), buf(144, 128), buf(1, 120), buf(1, 48192),
            buf(144, 128), buf(144, 128), buf(144, 128), buf(1, 120), buf(1, 48192),
            buf(1, 1920), buf(3, 144, 128), buf(8, 8, 768), buf(8, 3072),
            buf(4, 128, 128), buf(4, 128, 128), buf(128, 128), buf(4, 112, 128), buf(4, 144, 128),
            buf(4, 64, ROWS), buf(4, 2, 32, 256), buf(4, 2, 32, 256),
            buf(256, 256), buf(256, 256), buf(4, 48, ROWS),
            buf(F, 8, 640), buf(F, 8, 640), buf(F, 8, 640), buf(F, 8, 640), buf(F, 48, ROWS),
            sem(16), sem(10), sem(G), sem(G), sem(G), sem(G), sem(G), sem(G), sem(G), sem(G), sem(G), sem(F), sem(F), sem(G), sem(G), sem(G),
            sem(F), sem(F), sem(4), sem(F), sem(F), sem(F),
        ],
        compiler_params=pltpu.CompilerParams(collective_id=0, has_side_effects=True, vmem_limit_bytes=60 * 2**20),
        name="outer_step",
    )(
        delta_attn.reshape(192, 96), delta_in[0], delta_out[0], delta_small, emb_left[0, 0].T, emb_right[0],
        anchor_attn.reshape(144, 128), anchor_in.reshape(144, 128), anchor_out.reshape(144, 128),
        anchor_small.reshape(1, 120), anchor_emb.reshape(1, 48192),
        moment_attn.reshape(144, 128), moment_in.reshape(144, 128), moment_out.reshape(144, 128),
        moment_small.reshape(1, 120), moment_emb.reshape(1, 48192),
    )
    outs = pl.pallas_call(
        write_out,
        out_shape=results,
        in_specs=[hbm] * 10,
        out_specs=(hbm,) * 10,
        scratch_shapes=[*(pltpu.VMEM(r.shape, f32) for r in results), sem(10), sem(10)],
        compiler_params=pltpu.CompilerParams(vmem_limit_bytes=60 * 2**20),
        name="write_out",
    )(*held)
    return (
        outs[0].reshape(4, 48, 96), outs[1], outs[2], outs[3].reshape(1920), outs[4].T,
        outs[5].reshape(1, 18432), outs[6].reshape(1, 18432), outs[7].reshape(1, 18432),
        outs[8].reshape(120), outs[9].reshape(1, 1, 1, 48192),
    )


def solution(mesh):
    placed = (
        P("rep", None, "fsdp", "tp"),
        P("rep", "fsdp", "tp"),
        P("rep", "fsdp", "tp"),
        P("rep", None),
        P("rep", "tp", "fsdp", None),
        P("rep", None, None),
        P("tp", "fsdp"),
        P("tp", "fsdp"),
        P("tp", "fsdp"),
        P("fsdp"),
        P("tp", "fsdp", "rep", None),
        P("tp", "fsdp"),
        P("tp", "fsdp"),
        P("tp", "fsdp"),
        P("fsdp"),
        P("tp", "fsdp", "rep", None),
    )
    return jax.shard_map(
        on_device,
        mesh=mesh,
        in_specs=placed,
        out_specs=(
            P(None, "fsdp", "tp"),
            P("fsdp", "tp"),
            P("fsdp", "tp"),
            P(),
            P("tp", "fsdp"),
            P("tp", "fsdp"),
            P("tp", "fsdp"),
            P("tp", "fsdp"),
            P("fsdp"),
            P("tp", "fsdp", "rep", None),
        ),
        check_vma=False,
    )
```

```python
import jax
import jax.numpy as jnp
from jax import lax
from jax.experimental import pallas as pl
from jax.experimental.pallas import tpu as pltpu
from jax.sharding import PartitionSpec as P

OUTER_RATE = 0.7
MOMENTUM_COEF = 0.9
G = 4
F = 16
ROWS = 251
KEEP = OUTER_RATE * MOMENTUM_COEF * MOMENTUM_COEF
STEP = OUTER_RATE * (1.0 + MOMENTUM_COEF) / G
MEAN = 1.0 / G


def dot(a, b, ca, cb):
    return lax.dot_general(
        a, b, (((ca,), (cb,)), ((), ())), precision=lax.Precision.HIGHEST, preferred_element_type=jnp.float32
    )


def sixth(d):
    return (d * 43) >> 8


def spread_rows():
    row = lax.broadcasted_iota(jnp.int32, (128, 96), 0)
    col = lax.broadcasted_iota(jnp.int32, (128, 96), 1)
    return (row == col + 2 * sixth(col)).astype(jnp.float32)


def pick_columns(q):
    row = lax.broadcasted_iota(jnp.int32, (384, 96), 0)
    col = lax.broadcasted_iota(jnp.int32, (384, 96), 1)
    return (row == col + 18 * sixth(col) + 6 * q).astype(jnp.float32)


def kernel(
    d_attn_h, d_in_h, d_out_h, d_small_h, left_h, right_h,
    a_attn_h, a_in_h, a_out_h, a_small_h, a_emb_h,
    m_attn_h, m_in_h, m_out_h, m_small_h, m_emb_h,
    new_attn_h, new_in_h, new_out_h, new_small_h, new_emb_h,
    next_attn_h, next_in_h, next_out_h, next_small_h, next_emb_h,
    new_attn, new_in, new_out, new_small, new_emb,
    next_attn, next_in, next_out, next_small, next_emb,
    d_attn, d_in, d_out, d_small, right,
    a_attn, a_in, a_out, a_small, a_emb,
    m_attn, m_in, m_out, m_small, m_emb,
    flat_small, lin, wide, widef, quart, quart_in, own_sum, sums, tot, lts, rts_own, rts, base, un, et,
    amsg, arecv, umsg, urecv, gath,
    in_s, out_s, q_ss, q_rs, l_ss, l_rs, r_ss, r_rs, x_ss, x_rs, a_ss, a_rs, s_ss, s_rs, u_ss, u_rs, e_ss, up_ss, dn_ss, e_rs,
):
    f = lax.axis_index("fsdp")
    g = lax.axis_index("rep")
    c = lax.rem(f, 2)

    def peer_f(d):
        return lax.rem(f + d, F)

    def peer_g(d):
        return lax.rem(g + d, G)

    loads = [
        pltpu.make_async_copy(src, dst, in_s.at[i])
        for i, (src, dst) in enumerate((
            (left_h, lts.at[g]), (right_h, right), (d_in_h, d_in), (d_attn_h, d_attn), (d_out_h, d_out),
            (d_small_h, d_small), (a_attn_h, a_attn), (m_attn_h, m_attn), (a_out_h, a_out), (m_out_h, m_out),
            (a_in_h, a_in), (m_in_h, m_in), (a_small_h, a_small), (m_small_h, m_small), (a_emb_h, a_emb),
            (m_emb_h, m_emb),
        ))
    ]
    for load in loads:
        load.start()
    stores = [
        pltpu.make_async_copy(src, dst, out_s.at[i])
        for i, (src, dst) in enumerate((
            (new_attn, new_attn_h), (new_in, new_in_h), (new_out, new_out_h), (new_small, new_small_h),
            (new_emb, new_emb_h), (next_attn, next_attn_h), (next_in, next_in_h), (next_out, next_out_h),
            (next_small, next_small_h), (next_emb, next_emb_h),
        ))
    ]

    bar = pltpu.get_barrier_semaphore()

    @pl.loop(1, F)
    def _(d):
        pl.semaphore_signal(bar, inc=1, device_id={"fsdp": peer_f(d)}, device_id_type=pl.DeviceIdType.MESH)

    @pl.loop(1, G)
    def _(d):
        pl.semaphore_signal(bar, inc=1, device_id={"rep": peer_g(d)}, device_id_type=pl.DeviceIdType.MESH)

    for load in loads[:6]:
        load.wait()
    for q in range(G):
        for h in range(2):
            rts_own[q, h, :, 0:192] = right[h * 32 : (h + 1) * 32, q * 192 : (q + 1) * 192]
    rts[g] = rts_own[g]

    for t in range(F):
        quart[0, 112 + t : 113 + t, 0:120] = d_small[:, t * 120 : (t + 1) * 120]
    small = quart[0, 112:128, 0:120]
    x_in = d_in[...]
    for q in range(G):
        x_q = dot(x_in, pick_columns(q), 1, 0)
        quart[q, 0:48, 0:96] = d_attn[q * 48 : (q + 1) * 48, :]
        quart[q, 0:48, 96:128] = x_q[:, 0:32]
        quart[q, 48:96, 0:96] = d_out[q * 48 : (q + 1) * 48, :]
        quart[q, 48:96, 96:128] = x_q[:, 32:64]
        for b in range(3):
            quart[q, 96:112, b * 32 : (b + 1) * 32] = x_q[b * 16 : (b + 1) * 16, 64:96]
        if q:
            quart[q, 112:128, 0:120] = small
    quart_in[g] = quart[g]

    pl.semaphore_wait(bar, F + G - 2)

    def rep_copy(src, dst, ss, rs, d):
        return pltpu.make_async_remote_copy(
            src_ref=src, dst_ref=dst, send_sem=ss.at[d], recv_sem=rs.at[d],
            device_id={"rep": peer_g(d)}, device_id_type=pl.DeviceIdType.MESH)

    def left_copy(d):
        return rep_copy(lts.at[g], lts.at[g], l_ss, l_rs, d)

    def right_copy(d):
        return rep_copy(rts_own.at[peer_g(d), c], rts.at[g, c], r_ss, r_rs, d)

    def quarter_copy(d):
        return rep_copy(quart.at[peer_g(d)], quart_in.at[g], q_ss, q_rs, d)

    def sum_copy(d):
        return rep_copy(own_sum.at[pl.ds(0, 112)], sums.at[g], s_ss, s_rs, d)

    def half_copy(d):
        part = rts.at[peer_g(G - d), c]
        return pltpu.make_async_remote_copy(
            src_ref=part, dst_ref=part, send_sem=x_ss.at[d], recv_sem=x_rs.at[d],
            device_id={"fsdp": f + 1 - 2 * c}, device_id_type=pl.DeviceIdType.MESH)

    def anchor_copy(d):
        return pltpu.make_async_remote_copy(
            src_ref=amsg.at[peer_f(d)], dst_ref=arecv.at[f], send_sem=a_ss.at[d], recv_sem=a_rs.at[d],
            device_id={"fsdp": peer_f(d)}, device_id_type=pl.DeviceIdType.MESH)

    def total_copy(d):
        return pltpu.make_async_remote_copy(
            src_ref=umsg.at[peer_f(d)], dst_ref=urecv.at[f], send_sem=u_ss.at[d], recv_sem=u_rs.at[d],
            device_id={"fsdp": peer_f(d)}, device_id_type=pl.DeviceIdType.MESH)

    def each(copy, n, what):
        @pl.loop(1, n)
        def _(d):
            getattr(copy(d), what)()

    each(right_copy, G, "start")
    each(left_copy, G, "start")
    each(quarter_copy, G, "start")

    for load in loads[6:]:
        load.wait()

    @pl.loop(0, 125, unroll=5)
    def _(p):
        at = pl.ds(pl.multiple_of(p * 384, 128), 384)
        x = a_emb[:, at] - KEEP * m_emb[:, at]
        base[pl.ds(2 * p, 1), 0:192] = x[:, 0:192]
        base[pl.ds(2 * p + 1, 1), 0:192] = x[:, 192:384]

    base[250:251, 0:192] = a_emb[:, 48000:48192] - KEEP * m_emb[:, 48000:48192]

    @pl.loop(1, G)
    def _(d):
        right_copy(d).wait_recv()
        half_copy(d).start()

    amsg[...] = jnp.zeros((F, 8, 640), jnp.float32)
    lin[0] = a_attn[...] - KEEP * m_attn[...]
    lin[1] = a_out[...] - KEEP * m_out[...]
    lin[2] = a_in[...] - KEEP * m_in[...]
    for q in range(G):
        for s in range(6):
            wide[q, 0:6, s * 128 : (s + 1) * 128] = lin[0, pl.ds(q * 6 + s, 6, stride=24), :]
            wide[4 + q, 0:6, s * 128 : (s + 1) * 128] = lin[2, pl.ds(q * 36 + s, 6, stride=6), :]
    for s in range(24):
        widef[0:6, s * 128 : (s + 1) * 128] = lin[1, pl.ds(s, 6, stride=24), :]
    share = a_small[...] - KEEP * m_small[...]
    for t in range(F):
        for q in range(G):
            amsg[t, 0:6, q * 144 : q * 144 + 48] = wide[q, 0:6, t * 48 : (t + 1) * 48]
            amsg[t, 0:6, q * 144 + 48 : q * 144 + 96] = widef[0:6, t * 192 + q * 48 : t * 192 + q * 48 + 48]
            amsg[t, 0:6, q * 144 + 96 : q * 144 + 144] = wide[4 + q, 0:6, t * 48 : (t + 1) * 48]
        amsg[t, 6:7, 0:120] = share
    arecv[f] = amsg[f]
    each(anchor_copy, F, "start")

    each(left_copy, G, "wait_recv")
    each(half_copy, G, "wait_recv")
    u_emb = dot(lts[...].reshape(256, ROWS), rts[...].reshape(256, 256)[:, 0:192], 0, 0)
    un[0:ROWS, 0:192] = u_emb
    base[0:ROWS, 0:192] = base[0:ROWS, 0:192] - STEP * u_emb
    et[...] = jnp.transpose(base[...])[0:192, 0:ROWS].reshape(4, 48, ROWS)

    def emb_copy(i):
        return pltpu.make_async_remote_copy(
            src_ref=et.at[i], dst_ref=gath.at[f], send_sem=e_ss.at[i], recv_sem=e_rs.at[f],
            device_id={"fsdp": g * 4 + i}, device_id_type=pl.DeviceIdType.MESH)

    plane = lax.div(f, 4)

    @pl.loop(0, 4)
    def _(i):
        @pl.when(f != g * 4 + i)
        def _():
            emb_copy(i).start()

    @pl.when(plane == g)
    def _():
        gath[f] = et[lax.rem(f, 4)]

    each(quarter_copy, G, "wait_recv")
    own_sum[...] = quart_in[0] + quart_in[1] + quart_in[2] + quart_in[3]
    sums[g] = own_sum[0:112, :]
    each(sum_copy, G, "start")

    @pl.loop(0, 125, unroll=5)
    def _(p):
        at = pl.ds(pl.multiple_of(p * 384, 128), 384)
        x = jnp.concatenate([un[pl.ds(2 * p, 1), 0:192], un[pl.ds(2 * p + 1, 1), 0:192]], axis=1)
        next_emb[:, at] = MOMENTUM_COEF * m_emb[:, at] + MEAN * x

    next_emb[:, 48000:48192] = MOMENTUM_COEF * m_emb[:, 48000:48192] + MEAN * un[250:251, 0:192]
    stores[9].start()

    each(sum_copy, G, "wait_recv")
    for q in range(G):
        tot[q, 0:96, 0:96] = sums[q, 0:96, 0:96]
        tot[q, 96:144, 0:32] = sums[q, 0:48, 96:128]
        tot[q, 96:144, 32:64] = sums[q, 48:96, 96:128]
        for b in range(3):
            tot[q, 96 + b * 16 : 112 + b * 16, 64:96] = sums[q, 96:112, b * 32 : (b + 1) * 32]
    total = tot[...].reshape(576, 128)[:, 0:96]
    spread = spread_rows()
    umsg[:, :, 0:576] = dot(spread, total, 1, 1).reshape(F, 8, 576)
    urecv[f] = umsg[f]
    each(total_copy, F, "start")

    up = jnp.logical_and(g >= plane, g < G - 1)
    down = jnp.logical_and(g <= plane, g > 0)

    def up_copy(s):
        return pltpu.make_async_remote_copy(
            src_ref=gath.at[s], dst_ref=gath.at[s], send_sem=up_ss.at[s], recv_sem=e_rs.at[s],
            device_id={"rep": jnp.minimum(g + 1, G - 1)}, device_id_type=pl.DeviceIdType.MESH)

    def down_copy(s):
        return pltpu.make_async_remote_copy(
            src_ref=gath.at[s], dst_ref=gath.at[s], send_sem=dn_ss.at[s], recv_sem=e_rs.at[s],
            device_id={"rep": jnp.maximum(g - 1, 0)}, device_id_type=pl.DeviceIdType.MESH)

    def relay(lo, hi):
        @pl.loop(lo, hi)
        def _(k):
            s = peer_f(k)

            @pl.when(jnp.logical_or(plane != g, s != f))
            def _():
                up_copy(s).wait_recv()

            @pl.when(up)
            def _():
                up_copy(s).start()

            @pl.when(down)
            def _():
                down_copy(s).start()

    relay(0, 6)

    each(anchor_copy, F, "wait_recv")
    fixed = dot(arecv[...].reshape(128, 640)[:, 0:576], spread, 0, 0)
    fresh = fixed - STEP * total
    acc = jnp.zeros((48, 384), jnp.float32)
    for q in range(G):
        new_attn[q * 48 : (q + 1) * 48, :] = fresh[q * 144 : q * 144 + 48, :]
        new_out[q * 48 : (q + 1) * 48, :] = fresh[q * 144 + 48 : q * 144 + 96, :]
        acc = acc + dot(fresh[q * 144 + 96 : q * 144 + 144, :], pick_columns(q), 1, 1)
    new_in[...] = acc
    for t in range(F):
        flat_small[:, t * 120 : (t + 1) * 120] = arecv[t, 6:7, 0:120] - STEP * own_sum[112 + t : 113 + t, 0:120]
    for t in range(15):
        new_small[t : t + 1, :] = flat_small[:, t * 128 : (t + 1) * 128]
    next_small[...] = MOMENTUM_COEF * m_small[...] + MEAN * own_sum[pl.ds(112 + f, 1), 0:120]
    for i in (0, 1, 2, 3, 8):
        stores[i].start()

    relay(6, F)

    each(total_copy, F, "wait_recv")
    for t in range(F):
        for q in range(G):
            wide[q, :, t * 48 : (t + 1) * 48] = urecv[t, :, q * 144 : q * 144 + 48]
            widef[:, t * 192 + q * 48 : t * 192 + q * 48 + 48] = urecv[t, :, q * 144 + 48 : q * 144 + 96]
            wide[4 + q, :, t * 48 : (t + 1) * 48] = urecv[t, :, q * 144 + 96 : q * 144 + 144]
    for q in range(G):
        for s in range(6):
            lin[0, pl.ds(q * 6 + s, 6, stride=24), :] = wide[q, 0:6, s * 128 : (s + 1) * 128]
            lin[2, pl.ds(q * 36 + s, 6, stride=6), :] = wide[4 + q, 0:6, s * 128 : (s + 1) * 128]
    for s in range(24):
        lin[1, pl.ds(s, 6, stride=24), :] = widef[0:6, s * 128 : (s + 1) * 128]
    next_attn[...] = MOMENTUM_COEF * m_attn[...] + MEAN * lin[0]
    next_out[...] = MOMENTUM_COEF * m_out[...] + MEAN * lin[1]
    next_in[...] = MOMENTUM_COEF * m_in[...] + MEAN * lin[2]
    for i in (5, 6, 7):
        stores[i].start()

    for s in range(F):
        new_emb[:, s * ROWS : (s + 1) * ROWS] = gath[s]
    stores[4].start()

    each(left_copy, G, "wait_send")
    each(right_copy, G, "wait_send")
    each(half_copy, G, "wait_send")
    each(quarter_copy, G, "wait_send")
    each(sum_copy, G, "wait_send")
    each(anchor_copy, F, "wait_send")
    each(total_copy, F, "wait_send")

    @pl.loop(0, 4)
    def _(i):
        @pl.when(f != g * 4 + i)
        def _():
            emb_copy(i).wait_send()

    @pl.loop(0, F)
    def _(s):
        @pl.when(up)
        def _():
            up_copy(s).wait_send()

        @pl.when(down)
        def _():
            down_copy(s).wait_send()

    for store in stores:
        store.wait()


def write_out(*refs):
    n = (len(refs) - 2) // 3
    took, gave = refs[3 * n], refs[3 * n + 1]
    inward = [pltpu.make_async_copy(refs[i], refs[2 * n + i], took.at[i]) for i in range(n)]
    outward = [pltpu.make_async_copy(refs[2 * n + i], refs[n + i], gave.at[i]) for i in range(n)]
    for copy in inward:
        copy.start()
    for i in range(n):
        inward[i].wait()
        outward[i].start()
    for copy in outward:
        copy.wait()


def on_device(
    delta_attn, delta_in, delta_out, delta_small, emb_left, emb_right,
    anchor_attn, anchor_in, anchor_out, anchor_small, anchor_emb,
    moment_attn, moment_in, moment_out, moment_small, moment_emb,
):
    f32 = jnp.float32
    shape = lambda *s: jax.ShapeDtypeStruct(s, f32)
    hbm = pl.BlockSpec(memory_space=pltpu.HBM)
    buf = lambda *s: pltpu.VMEM(s, f32)
    sem = lambda n: pltpu.SemaphoreType.DMA((n,))
    results = (
        shape(192, 96), shape(48, 384), shape(192, 96), shape(15, 128), shape(48, 4016),
        shape(144, 128), shape(144, 128), shape(144, 128), shape(1, 120), shape(1, 48192),
    )
    held = pl.pallas_call(
        kernel,
        out_shape=results,
        in_specs=[hbm] * 16,
        out_specs=(hbm,) * 10,
        scratch_shapes=[
            *(pltpu.VMEM(r.shape, f32) for r in results),
            buf(192, 96), buf(48, 384), buf(192, 96), buf(1, 1920), buf(64, 768),
            buf(144, 128), buf(144, 128), buf(144, 128), buf(1, 120), buf(1, 48192),
            buf(144, 128), buf(144, 128), buf(144, 128), buf(1, 120), buf(1, 48192),
            buf(1, 1920), buf(3, 144, 128), buf(8, 8, 768), buf(8, 3072),
            buf(4, 128, 128), buf(4, 128, 128), buf(128, 128), buf(4, 112, 128), buf(4, 144, 128),
            buf(4, 64, ROWS), buf(4, 2, 32, 256), buf(4, 2, 32, 256),
            buf(256, 256), buf(256, 256), buf(4, 48, ROWS),
            buf(F, 8, 640), buf(F, 8, 640), buf(F, 8, 640), buf(F, 8, 640), buf(F, 48, ROWS),
            sem(16), sem(10), sem(G), sem(G), sem(G), sem(G), sem(G), sem(G), sem(G), sem(G), sem(F), sem(F), sem(G), sem(G),
            sem(F), sem(F), sem(4), sem(F), sem(F), sem(F),
        ],
        compiler_params=pltpu.CompilerParams(collective_id=0, has_side_effects=True, vmem_limit_bytes=60 * 2**20),
        name="outer_step",
    )(
        delta_attn.reshape(192, 96), delta_in[0], delta_out[0], delta_small, emb_left[0, 0].T, emb_right[0],
        anchor_attn.reshape(144, 128), anchor_in.reshape(144, 128), anchor_out.reshape(144, 128),
        anchor_small.reshape(1, 120), anchor_emb.reshape(1, 48192),
        moment_attn.reshape(144, 128), moment_in.reshape(144, 128), moment_out.reshape(144, 128),
        moment_small.reshape(1, 120), moment_emb.reshape(1, 48192),
    )
    outs = pl.pallas_call(
        write_out,
        out_shape=results,
        in_specs=[hbm] * 10,
        out_specs=(hbm,) * 10,
        scratch_shapes=[*(pltpu.VMEM(r.shape, f32) for r in results), sem(10), sem(10)],
        compiler_params=pltpu.CompilerParams(vmem_limit_bytes=60 * 2**20),
        name="write_out",
    )(*held)
    return (
        outs[0].reshape(4, 48, 96), outs[1], outs[2], outs[3].reshape(1920), outs[4].T,
        outs[5].reshape(1, 18432), outs[6].reshape(1, 18432), outs[7].reshape(1, 18432),
        outs[8].reshape(120), outs[9].reshape(1, 1, 1, 48192),
    )


def solution(mesh):
    placed = (
        P("rep", None, "fsdp", "tp"),
        P("rep", "fsdp", "tp"),
        P("rep", "fsdp", "tp"),
        P("rep", None),
        P("rep", "tp", "fsdp", None),
        P("rep", None, None),
        P("tp", "fsdp"),
        P("tp", "fsdp"),
        P("tp", "fsdp"),
        P("fsdp"),
        P("tp", "fsdp", "rep", None),
        P("tp", "fsdp"),
        P("tp", "fsdp"),
        P("tp", "fsdp"),
        P("fsdp"),
        P("tp", "fsdp", "rep", None),
    )
    return jax.shard_map(
        on_device,
        mesh=mesh,
        in_specs=placed,
        out_specs=(
            P(None, "fsdp", "tp"),
            P("fsdp", "tp"),
            P("fsdp", "tp"),
            P(),
            P("tp", "fsdp"),
            P("tp", "fsdp"),
            P("tp", "fsdp"),
            P("tp", "fsdp"),
            P("fsdp"),
            P("tp", "fsdp", "rep", None),
        ),
        check_vma=False,
    )
```
